128 devices in a mesh: grp: 8 (over y, core), tile: 16 (over z, x).
Axes of the slice: x: 4, y: 4, z: 4, core: 2. Of those that a mesh axis runs over, the one named last changes fastest.
Arguments:
- coefficient_array: bfloat16 [2097152, 256], P(('grp', 'tile')), may hold values from -6 to 6
- prior_thermal_field: bfloat16 [524288, 256], P(('grp', 'tile')), may hold values from -6 to 6
- gauge_cable_position: int32 [65536], P(('grp', 'tile')), may hold values from 0 to 4095
- gauge_damping_bucket: int32 [65536, 1], P(('grp', 'tile')), may hold values from 0 to 7; in each aligned block of 512 rows (0 to 511, 512 to 1023, ...) at most 128 rows name the same one
- gauge_misfit_sigma: float32 [65536], P(('grp', 'tile')), may hold values from 1 to 6
- jittered_observations: bfloat16 [65536, 256], P(('grp', 'tile')), may hold values from -12 to 12
Outputs:
- updated: bfloat16 [2097152, 256], P(('grp', 'tile'))
The draws below stay inside these ranges and needn't reach their ends.
Inputs may be any that keep to these rules, and one draw needn't show every extreme that they name: `gauge_damping_bucket`: of the sensors of one device, at most 128 belong to one group.
All inputs are finite; a program needn't handle non-finite values.
Results may differ from the reference program's by a relative error of at most 0.0093.
Values may be sent and summed in bfloat16 or wider, within the bound.
A program may use at most 64 MiB of HBM per device.

```python
import math
import jax
import jax.numpy as jnp
import numpy as np
from jax import lax

REALIZATION_NUM = 256
P_DEV = 16384
CELLS_DEV = 4096
S_DEV = 512
CAP = 128
NPAR = 2097152
MESH_SITE_NUMBER = 524288
NSENS = 65536
N_GRP = 8
N_TILE = 16


def rough_field(key, rows, spread, bound):
    values = jax.random.normal(key, (rows, REALIZATION_NUM), jnp.float32)
    return jnp.clip(values * spread, -bound, bound)


def draw_prior_thermal_field(key, part):
    return rough_field(jax.random.fold_in(key, 11), MESH_SITE_NUMBER, 1.0, 6.0).astype(jnp.bfloat16)


def draw_jittered_observations(key, part):
    return rough_field(jax.random.fold_in(key, 23), NSENS, 2.0, 12.0).astype(jnp.bfloat16)


def place_ends(array, stream_key, low, high):
    spot = [jax.random.randint(jax.random.fold_in(stream_key, axis), (), 0, length) for axis, length in enumerate(array.shape)]
    main_axis = array.shape.index(max(array.shape))
    next_to = spot[:main_axis] + [(spot[main_axis] + 1) % array.shape[main_axis]] + spot[main_axis + 1:]
    return array.at[tuple(spot)].set(low).at[tuple(next_to)].set(high)


def steps_of(rng, dims, cuts, smallest, top_value):
    def one(dim, shards_of):
        heights = jax.random.uniform(jax.random.fold_in(jax.random.fold_in(rng, 6), dim), (shards_of,), jnp.float32, smallest / len(cuts), top_value / len(cuts))
        return jnp.repeat(jnp.exp(heights), dims[dim] // shards_of).reshape((-1,) + (1,) * (len(dims) - dim - 1))

    level = one(*cuts[0])
    for cut in cuts[1:]:
        level = level * one(*cut)
    return level


def shared_out(rng, own, number, rows, number_of, top, limit, slope):
    order = jax.random.permutation(rng, number_of)
    heavy_load, ordinary = shares(number_of, rows * top, limit, slope, True), shares(number_of, rows * top, limit, slope, False)
    places = jnp.arange(number_of)

    def named(lengths, rotation):
        used = int((lengths > 0).sum())
        fixed = max(1, used // 4)
        shifted = fixed + (places - fixed + rotation * (used - fixed)) % max(1, number_of - fixed)
        return jnp.zeros((number_of,), jnp.int32).at[order[jnp.where(places < fixed, places, shifted)]].set(jnp.asarray(lengths, jnp.int32))

    lengths = jnp.where(number % 4 == 0, named(heavy_load, number // 4), named(ordinary, number - number // 4 - 1))
    mixed = jax.random.permutation(jax.random.fold_in(own, 3), number_of)
    giver, receiver = mixed[0:number_of // 2 * 2:2], mixed[1:number_of // 2 * 2:2]
    slack = jnp.minimum(lengths[giver] - 1, limit - lengths[receiver]) // 2
    slack = jnp.where((giver == order[0]) | (receiver == order[0]) | (lengths[receiver] == 0), 0, jnp.maximum(slack, 0))
    shifted = jax.random.randint(jax.random.fold_in(own, 4), (number_of // 2,), 0, 1 << 20) % (slack + 1)
    lengths = lengths.at[giver].add(-shifted).at[receiver].add(shifted)
    labels = jnp.searchsorted(jnp.cumsum(lengths), jnp.arange(rows * top), side="right").astype(jnp.int32)
    listing = labels.reshape(top, rows).T
    listing = listing[jax.random.permutation(jax.random.fold_in(own, 1), rows)]
    rotation = jax.random.randint(jax.random.fold_in(own, 2), (rows, 1), 0, top)
    return jnp.take_along_axis(listing, (jnp.arange(top)[None, :] + rotation) % top, axis=1)


def shares(number_of, total, reach, skew, full):
    portions = [(1 << 20) // math.isqrt(rank ** skew) + 1 for rank in range(1, number_of + 1)]
    largest = reach if full else min(reach, max(-(-total // number_of), total * portions[0] // sum(portions)))
    least = 1 if total - largest >= number_of - 1 else 0
    holding, surplus = [largest] + [least] * (number_of - 1), total - largest - least * (number_of - 1)
    while surplus > 0:
        candidates = [i for i in range(1, number_of) if holding[i] < largest] or [i for i in range(1, number_of) if holding[i] < reach]
        whole, remaining = sum([portions[i] for i in candidates]), surplus
        for i in candidates:
            extra = min(reach - holding[i], max(1, remaining * portions[i] // whole), surplus)
            holding[i] = holding[i] + extra
            surplus = surplus - extra
    return np.array(holding)


def normal_values(own_key, extent, width, limit, cuts=(), kind=jnp.bfloat16):
    entries = width * jax.random.normal(own_key, extent, jnp.float32)
    if cuts:
        entries = entries * steps_of(own_key, extent, cuts, -0.22, 0.18)
    return jnp.clip(entries, -limit, limit).astype(kind)


def setup_inputs(seed: int = 0) -> dict:
    arg_keys = jax.random.split(jax.random.key(seed), 7)
    coefficient_array = normal_values(arg_keys[0], (NPAR, REALIZATION_NUM), 1.0, 6.0, ((0, 128),))
    prior_thermal_field = draw_prior_thermal_field(jax.random.fold_in(arg_keys[6], 71), 0)
    gauge_cable_position = place_ends(jax.random.randint(arg_keys[2], (NSENS,), 0, CELLS_DEV), jax.random.fold_in(arg_keys[2], 1), 0, CELLS_DEV - 1).astype(jnp.int32)
    gauge_damping_bucket_keys = jax.random.split(jax.random.fold_in(arg_keys[3], 1), NSENS // S_DEV)
    gauge_damping_bucket_turns = jax.random.permutation(jax.random.fold_in(arg_keys[3], 3), NSENS // S_DEV)
    gauge_damping_bucket = jax.vmap(lambda own, number: shared_out(jax.random.fold_in(arg_keys[3], 2), own, number, S_DEV, N_GRP, 1, CAP, 2))(gauge_damping_bucket_keys, gauge_damping_bucket_turns).reshape((NSENS, 1))
    gauge_misfit_sigma = jnp.clip(jnp.exp(math.log(6.0) - 1.7917595 * jax.random.uniform(arg_keys[4], (NSENS,), jnp.float32) ** steps_of(arg_keys[4], (NSENS,), ((0, 128),), -0.2, 0.2)), 1.0, 6.0)
    jittered_observations = draw_jittered_observations(jax.random.fold_in(arg_keys[6], 71), 0)
    return dict(coefficient_array=coefficient_array, prior_thermal_field=prior_thermal_field, gauge_cable_position=gauge_cable_position, gauge_damping_bucket=gauge_damping_bucket, gauge_misfit_sigma=gauge_misfit_sigma, jittered_observations=jittered_observations)


def solve_group(gram, cross):
    factor = jnp.linalg.cholesky(gram + jnp.eye(gram.shape[0], dtype=jnp.float32))
    return jax.scipy.linalg.cho_solve((factor, True), cross)

def reference(coefficient_array, prior_thermal_field, gauge_cable_position, gauge_damping_bucket, gauge_misfit_sigma, jittered_observations):
    members = coefficient_array.shape[1]
    root_scale = math.sqrt(members - 1)
    owner = jnp.arange(NSENS, dtype=jnp.int32) // S_DEV
    mesh_index_list = (owner * CELLS_DEV + gauge_cable_position).astype(jnp.int32)
    kept_indices = prior_thermal_field[mesh_index_list].astype(jnp.float32)
    member_mean = lax.optimization_barrier(jnp.mean(kept_indices, axis=1, keepdims=True))
    scaled = ((kept_indices - member_mean) / (gauge_misfit_sigma[:, None] * root_scale)).astype(jnp.bfloat16)
    misfit = ((jittered_observations.astype(jnp.float32) - kept_indices) / gauge_misfit_sigma[:, None]).astype(jnp.bfloat16)
    group_ids = gauge_damping_bucket[:, 0]

    def per_group(group):
        inside = (group_ids == group)[:, None]
        masked = jnp.where(inside, scaled, jnp.zeros_like(scaled))
        gram = jnp.dot(masked.T.astype(jnp.float32), masked.astype(jnp.float32), preferred_element_type=jnp.float32)
        cross = jnp.dot(masked.T.astype(jnp.float32), misfit.astype(jnp.float32), preferred_element_type=jnp.float32)
        return (solve_group(gram, cross) / root_scale).astype(jnp.bfloat16)
    transforms = lax.map(per_group, jnp.arange(N_GRP, dtype=jnp.int32))
    blocks = coefficient_array.reshape(N_GRP, N_TILE * P_DEV, members)

    def update(pair):
        block, transform = pair
        values = block.astype(jnp.float32)
        anomaly = (values - lax.optimization_barrier(jnp.mean(values, axis=1, keepdims=True))).astype(jnp.bfloat16)
        change = jnp.dot(anomaly.astype(jnp.float32), transform.astype(jnp.float32), preferred_element_type=jnp.float32)
        return (values + change).astype(jnp.bfloat16)
    return lax.map(update, (blocks, transforms)).reshape(coefficient_array.shape)
```

```python
import functools
import math

import jax
import jax.numpy as jnp
from jax import lax
from jax.experimental import pallas as pl
from jax.experimental.pallas import tpu as pltpu
from jax.sharding import PartitionSpec as P

F32, BF16 = jnp.float32, jnp.bfloat16
MESH = pl.DeviceIdType.MESH
VMEM = pl.BlockSpec(memory_space=pltpu.VMEM)
ANY = pl.BlockSpec(memory_space=pl.ANY)
BLOCK = 512
SAFE_BOUND = 256.0
ROW_TILE = 2048


def dot(a, b):
    return lax.dot_general(a, b, (((1,), (0,)), ((), ())), preferred_element_type=F32)


def dot_rows(a, b):
    return lax.dot_general(a, b, (((0,), (0,)), ((), ())), preferred_element_type=F32)


def split(a):
    high = a.astype(BF16)
    return high, (a - high.astype(F32)).astype(BF16)


def dot_split(a, b_high, b_low):
    a_high, a_low = split(a)
    return dot(a_high, b_high) + (dot(a_low, b_high) + dot(a_high, b_low))


def exchange(
    groups,
    tiles,
    position,
    bucket,
    sigma,
    field,
    observed,
    gram_out,
    cross_out,
    field_vmem,
    picked,
    send_scaled,
    send_misfit,
    got_scaled,
    got_misfit,
    part,
    pieces,
    mine,
    field_sem,
    send_sem,
    got_sem,
    piece_send,
    piece_got,
    whole_send,
    whole_got,
):
    cells, members = field.shape
    sensors = position.shape[1]
    capacity = send_scaled.shape[1]
    rows = members // tiles
    root_scale = math.sqrt(members - 1)
    my_group, my_tile = lax.axis_index("grp"), lax.axis_index("tile")

    def other_group(offset):
        return lax.rem(my_group + offset, groups)

    def other_tile(offset):
        return lax.rem(my_tile + offset, tiles)

    loads = []
    for block in range(cells // BLOCK):
        part_rows = pl.ds(block * BLOCK, BLOCK)
        loads.append(
            pltpu.make_async_copy(field.at[part_rows], field_vmem.at[part_rows], field_sem.at[block])
        )
        loads[-1].start()

    barrier = pltpu.get_barrier_semaphore()
    for offset in range(1, groups):
        pl.semaphore_signal(
            barrier, inc=1, device_id={"grp": other_group(offset)}, device_id_type=MESH
        )
    for offset in range(1, tiles):
        pl.semaphore_signal(
            barrier, inc=1, device_id={"tile": other_tile(offset)}, device_id_type=MESH
        )

    cell = position[...]
    group = bucket[...]
    facts = jnp.concatenate(
        [cell.astype(F32), sigma[...], jnp.zeros((6, sensors), F32)], axis=0
    ).T
    cell_column, sigma_column = facts[:, 0:1].astype(jnp.int32), facts[:, 1:2]

    lane = lax.broadcasted_iota(jnp.int32, (sensors, sensors), 1)
    row = lax.broadcasted_iota(jnp.int32, (sensors, sensors), 0)
    earlier = (row < lane).astype(F32).astype(BF16)
    member_of = (lax.broadcasted_iota(jnp.int32, (groups, sensors), 0) == group).astype(F32)
    before = dot(member_of.astype(BF16), earlier)
    rank = jnp.sum(before * member_of, axis=0, keepdims=True).astype(jnp.int32)
    target = group * capacity + rank

    for block in range(cells // BLOCK):
        part_rows = pl.ds(block * BLOCK, BLOCK)
        chosen = (
            lax.broadcasted_iota(jnp.int32, (sensors, BLOCK), 1) == cell_column - block * BLOCK
        )
        loads[block].wait()
        value = dot(chosen.astype(F32).astype(BF16), field_vmem[part_rows, :])
        if block == 0:
            picked[...] = value
        else:
            picked[...] += value

    kept = picked[...]
    mean = jnp.mean(kept, axis=1, keepdims=True)
    scaled = ((kept - mean) / (sigma_column * root_scale)).astype(BF16)
    misfit = ((observed[...].astype(F32) - kept) / sigma_column).astype(BF16)

    def place(values, offset):
        slot = other_group(offset) * capacity + lax.broadcasted_iota(
            jnp.int32, (capacity, sensors), 0
        )
        return dot((slot == target).astype(F32).astype(BF16), values).astype(BF16)

    def row_copy(source, landing, kind, offset):
        return pltpu.make_async_remote_copy(
            src_ref=source.at[offset],
            dst_ref=landing.at[offset],
            send_sem=send_sem.at[kind, offset],
            recv_sem=got_sem.at[kind, offset],
            device_id={"grp": other_group(offset)},
            device_id_type=MESH,
        )

    order = [4, 3, 5, 2, 6, 1, 7, 0]
    sends = []
    for kind, (values, buffer, landing) in enumerate(
        ((scaled, send_scaled, got_scaled), (misfit, send_misfit, got_misfit))
    ):
        ready = None
        for offset in order:
            buffer[offset] = place(values, offset)
            if kind == 0 and ready is None:
                pl.semaphore_wait(barrier, groups + tiles - 2)
            if ready is not None:
                ready.start()
                sends.append(ready)
            ready = row_copy(buffer, landing, kind, offset) if offset else None

    def piece_copy(which, offset):
        target_rows = pl.ds(pl.multiple_of(other_tile(offset) * rows, rows), rows)
        return pltpu.make_async_remote_copy(
            src_ref=part.at[which, target_rows],
            dst_ref=pieces.at[which, offset],
            send_sem=piece_send.at[which, offset],
            recv_sem=piece_got.at[which, offset],
            device_id={"tile": other_tile(offset)},
            device_id_type=MESH,
        )

    my_rows = pl.ds(pl.multiple_of(my_tile * rows, rows), rows)

    def whole_copy(which, out, offset):
        return pltpu.make_async_remote_copy(
            src_ref=mine.at[which],
            dst_ref=out.at[my_rows],
            send_sem=whole_send.at[which, offset],
            recv_sem=whole_got.at[which, offset],
            device_id={"tile": other_tile(offset)},
            device_id_type=MESH,
        )

    def whole_wait(which, out, offset):
        source = lax.rem(my_tile + tiles - offset, tiles)
        source_rows = pl.ds(pl.multiple_of(source * rows, rows), rows)
        pltpu.make_async_remote_copy(
            src_ref=mine.at[which],
            dst_ref=out.at[source_rows],
            send_sem=whole_send.at[which, offset],
            recv_sem=whole_got.at[which, offset],
            device_id={"tile": other_tile(offset)},
            device_id_type=MESH,
        ).wait_recv()

    def add_up(which, right_own, right_got):
        part[which] = dot_rows(send_scaled[0], right_own[0])
        for offset in order[:-1]:
            row_copy(send_scaled, got_scaled, which, offset).wait_recv()
            part[which] += dot_rows(got_scaled[offset], right_got[offset])
        for offset in range(1, tiles):
            piece_copy(which, offset).start()

    def spread(which, out):
        total = part[which, my_rows]
        for offset in range(1, tiles):
            piece_copy(which, offset).wait_recv()
            total = total + pieces[which, offset]
        mine[which] = total
        out[my_rows] = total
        for offset in range(1, tiles):
            whole_copy(which, out, offset).start()

    add_up(0, send_scaled, got_scaled)
    spread(0, gram_out)
    add_up(1, send_misfit, got_misfit)
    spread(1, cross_out)
    for which, out in ((0, gram_out), (1, cross_out)):
        for offset in range(1, tiles):
            whole_wait(which, out, offset)
    for copy in sends:
        copy.wait_send()
    for which, out in ((0, gram_out), (1, cross_out)):
        for offset in range(1, tiles):
            piece_copy(which, offset).wait_send()
            whole_copy(which, out, offset).wait_send()


def sums(groups, tiles, position, bucket, sigma, field, observed):
    cells, members = field.shape
    sensors = position.shape[1]
    capacity = sensors // 4
    rows = members // tiles
    return pl.pallas_call(
        functools.partial(exchange, groups, tiles),
        out_shape=[jax.ShapeDtypeStruct((members, members), F32)] * 2,
        in_specs=[VMEM, VMEM, VMEM, ANY, VMEM],
        out_specs=[VMEM, VMEM],
        scratch_shapes=[
            pltpu.VMEM((cells, members), BF16),
            pltpu.VMEM((sensors, members), F32),
            pltpu.VMEM((groups, capacity, members), BF16),
            pltpu.VMEM((groups, capacity, members), BF16),
            pltpu.VMEM((groups, capacity, members), BF16),
            pltpu.VMEM((groups, capacity, members), BF16),
            pltpu.VMEM((2, members, members), F32),
            pltpu.VMEM((2, tiles, rows, members), F32),
            pltpu.VMEM((2, rows, members), F32),
            pltpu.SemaphoreType.DMA((cells // BLOCK,)),
            pltpu.SemaphoreType.DMA((2, groups)),
            pltpu.SemaphoreType.DMA((2, groups)),
            pltpu.SemaphoreType.DMA((2, tiles)),
            pltpu.SemaphoreType.DMA((2, tiles)),
            pltpu.SemaphoreType.DMA((2, tiles)),
            pltpu.SemaphoreType.DMA((2, tiles)),
        ],
        compiler_params=pltpu.CompilerParams(
            collective_id=0, has_side_effects=True, vmem_limit_bytes=24 << 20
        ),
        name="sums",
    )(position, bucket, sigma, field, observed)


def apply(gram, cross, values, out, loaded, stored, inverse, power, transform, load_sem, store_sem):
    total_rows, members = values.shape
    steps = total_rows // ROW_TILE

    def load(step):
        part = pl.ds(step * ROW_TILE, ROW_TILE)
        return pltpu.make_async_copy(values.at[part], loaded.at[part], load_sem.at[step])

    for step in range(steps):
        load(step).start()

    identity = (
        lax.broadcasted_iota(jnp.int32, (members, members), 0)
        == lax.broadcasted_iota(jnp.int32, (members, members), 1)
    ).astype(F32)
    matrix = gram[...] + identity
    bound = jnp.max(jnp.sum(jnp.abs(matrix), axis=1, keepdims=True))

    @pl.when(bound <= SAFE_BOUND)
    def _():
        scale = 1.0 / bound
        power[...] = identity - matrix * scale
        inverse[...] = identity * scale

        def double(_, reach):
            high, low = split(power[...])
            now = inverse[...]
            inverse[...] = now + dot_split(now, high, low)
            power[...] = dot(high, high) + (dot(high, low) + dot(low, high))
            return reach * 2.0

        lax.while_loop(lambda reach: reach < bound * 14.0, lambda reach: double(0, reach), 1.0)
        now = inverse[...]
        high, low = split(now)
        rest = identity - dot_split(gram[...] + identity, high, low)
        rest_high, rest_low = split(rest)
        inverse[...] = now + dot_split(now, rest_high, rest_low)

    @pl.when(bound > SAFE_BOUND)
    def _():
        inverse[...] = matrix
        line = lax.broadcasted_iota(jnp.int32, (members, 1), 0)
        spot = lax.broadcasted_iota(jnp.int32, (1, members), 1)

        def eliminate(step, _):
            now = inverse[...]
            here, there = (line == step), (spot == step)
            row = jnp.sum(jnp.where(here, now, 0.0), axis=0, keepdims=True)
            column = jnp.sum(jnp.where(there, now, 0.0), axis=1, keepdims=True)
            pivot = jnp.sum(jnp.where(there, row, 0.0), axis=1, keepdims=True)
            row = jnp.where(there, 1.0, row) / pivot
            column = jnp.where(here, 0.0, column)
            base = jnp.where(there, 0.0, now)
            inverse[...] = jnp.where(here, row, base - column * row)
            return 0

        lax.fori_loop(0, members, eliminate, 0)

    high, low = split(cross[...])
    weights = dot_split(inverse[...], high, low)
    transform[...] = (weights / math.sqrt(members - 1)).astype(BF16)

    def store(step, slot):
        part = pl.ds(step * ROW_TILE, ROW_TILE)
        return pltpu.make_async_copy(stored.at[slot], out.at[part], store_sem.at[slot])

    for step in range(steps):
        slot = step % 2
        load(step).wait()
        now = loaded[pl.ds(step * ROW_TILE, ROW_TILE), :].astype(F32)
        anomaly = (now - jnp.mean(now, axis=1, keepdims=True)).astype(BF16)
        change = dot(anomaly, transform[...])
        if step >= 2:
            store(step - 2, slot).wait()
        stored[slot] = (now + change).astype(BF16)
        store(step, slot).start()
    for step in range(steps - 2, steps):
        store(step, step % 2).wait()


def update(gram, cross, values):
    total_rows, members = values.shape
    steps = total_rows // ROW_TILE
    return pl.pallas_call(
        apply,
        out_shape=jax.ShapeDtypeStruct(values.shape, values.dtype),
        in_specs=[VMEM, VMEM, ANY],
        out_specs=ANY,
        scratch_shapes=[
            pltpu.VMEM((total_rows, members), BF16),
            pltpu.VMEM((2, ROW_TILE, members), BF16),
            pltpu.VMEM((members, members), F32),
            pltpu.VMEM((members, members), F32),
            pltpu.VMEM((members, members), BF16),
            pltpu.SemaphoreType.DMA((steps,)),
            pltpu.SemaphoreType.DMA((2,)),
        ],
        compiler_params=pltpu.CompilerParams(vmem_limit_bytes=48 << 20),
        name="update",
    )(gram, cross, values)


def solution(mesh):
    groups, tiles = mesh.shape["grp"], mesh.shape["tile"]

    def shards(coefficients, field, position, bucket, sigma, observed):
        sensors = position.shape[0]
        gram, cross = sums(
            groups,
            tiles,
            position.reshape(1, sensors),
            bucket.reshape(1, sensors),
            sigma.reshape(1, sensors),
            field,
            observed,
        )
        return update(gram, cross, coefficients)

    rows, flat = P(("grp", "tile"), None), P(("grp", "tile"))
    return jax.shard_map(
        shards,
        mesh=mesh,
        in_specs=(rows, rows, flat, rows, flat, rows),
        out_specs=rows,
        check_vma=False,
    )
```

```python
import functools
import math

import jax
import jax.numpy as jnp
from jax import lax
from jax.experimental import pallas as pl
from jax.experimental.pallas import tpu as pltpu
from jax.sharding import PartitionSpec as P

F32, BF16 = jnp.float32, jnp.bfloat16
MESH = pl.DeviceIdType.MESH
VMEM = pl.BlockSpec(memory_space=pltpu.VMEM)
HBM = pl.BlockSpec(memory_space=pltpu.HBM)
BLOCK = 512
SAFE_BOUND = 512.0
STEPS = 8
ROW_TILE = 2048


def dot(a, b):
    return lax.dot_general(a, b, (((1,), (0,)), ((), ())), preferred_element_type=F32)


def dot_rows(a, b):
    return lax.dot_general(a, b, (((0,), (0,)), ((), ())), preferred_element_type=F32)


def split(a):
    high = a.astype(BF16)
    return high, (a - high.astype(F32)).astype(BF16)


def dot_split(a, b_high, b_low):
    a_high, a_low = split(a)
    return dot(a_high, b_high) + (dot(a_low, b_high) + dot(a_high, b_low))


def exchange(
    groups,
    tiles,
    position,
    bucket,
    sigma,
    field,
    observed,
    inverse_out,
    gram_out,
    cross_out,
    bound_out,
    position_vmem,
    bucket_vmem,
    sigma_vmem,
    observed_vmem,
    field_vmem,
    picked,
    send_rows,
    got_rows,
    gram_part,
    gram_pieces,
    gram_mine,
    gram_whole,
    cross_part,
    cross_pieces,
    cross_mine,
    pair,
    small_sem,
    field_sem,
    send_sem,
    got_sem,
    piece_send,
    piece_got,
    whole_send,
    whole_got,
):
    cells, members = field.shape
    sensors = position.shape[1]
    capacity = sensors // 4
    half = members // 2
    root_scale = math.sqrt(members - 1)
    my_group, my_tile = lax.axis_index("grp"), lax.axis_index("tile")
    ys, side = groups // 2, math.isqrt(tiles)

    def other_group(offset):
        far, core = offset // 2, offset % 2
        there = lax.rem(my_group // 2 + far, ys)
        return there * 2 + lax.rem(my_group + core, 2)

    def other_tile(offset, sign=1):
        far, near = offset // side, offset % side
        far, near = (far, near) if sign > 0 else (side - far, side - near)
        z = lax.rem(my_tile // side + far, side)
        return z * side + lax.rem(lax.rem(my_tile, side) + near, side)

    def ring(step, size):
        return min(step, size - step)

    tile_order = sorted(
        range(1, tiles), key=lambda o: -ring(o // side, side) - ring(o % side, side)
    )
    group_order = sorted(range(1, groups), key=lambda o: -ring(o // 2, ys))

    small = [
        pltpu.make_async_copy(source, landing, small_sem.at[number])
        for number, (source, landing) in enumerate(
            (
                (position, position_vmem),
                (bucket, bucket_vmem),
                (sigma, sigma_vmem),
                (observed, observed_vmem),
            )
        )
    ]
    for copy in small[:3]:
        copy.start()
    loads = []
    for block in range(cells // BLOCK):
        part_rows = pl.ds(block * BLOCK, BLOCK)
        loads.append(
            pltpu.make_async_copy(field.at[part_rows], field_vmem.at[part_rows], field_sem.at[block])
        )
        loads[-1].start()
    small[3].start()

    barrier = pltpu.get_barrier_semaphore()
    for offset in group_order:
        pl.semaphore_signal(
            barrier, inc=1, device_id={"grp": other_group(offset)}, device_id_type=MESH
        )
    for offset in tile_order:
        pl.semaphore_signal(
            barrier, inc=1, device_id={"tile": other_tile(offset)}, device_id_type=MESH
        )

    for copy in small[:3]:
        copy.wait()
    cell = position_vmem[...]
    group = bucket_vmem[...]
    facts = jnp.concatenate(
        [cell.astype(F32), sigma_vmem[...], jnp.zeros((6, sensors), F32)], axis=0
    ).T
    cell_column, sigma_column = facts[:, 0:1].astype(jnp.int32), facts[:, 1:2]

    lane = lax.broadcasted_iota(jnp.int32, (sensors, sensors), 1)
    row = lax.broadcasted_iota(jnp.int32, (sensors, sensors), 0)
    earlier = (row < lane).astype(F32).astype(BF16)
    member_of = (lax.broadcasted_iota(jnp.int32, (groups, sensors), 0) == group).astype(F32)
    before = dot(member_of.astype(BF16), earlier)
    rank = jnp.sum(before * member_of, axis=0, keepdims=True).astype(jnp.int32)
    target = group * capacity + rank

    for block in range(cells // BLOCK):
        part_rows = pl.ds(block * BLOCK, BLOCK)
        chosen = (
            lax.broadcasted_iota(jnp.int32, (sensors, BLOCK), 1) == cell_column - block * BLOCK
        )
        loads[block].wait()
        value = dot(chosen.astype(F32).astype(BF16), field_vmem[part_rows, :])
        if block == 0:
            picked[...] = value
        else:
            picked[...] += value

    kept = picked[...]
    mean = jnp.mean(kept, axis=1, keepdims=True)
    scaled = ((kept - mean) / (sigma_column * root_scale)).astype(BF16)
    small[3].wait()
    misfit = ((observed_vmem[...].astype(F32) - kept) / sigma_column).astype(BF16)

    def place(values, offset):
        slot = other_group(offset) * capacity + lax.broadcasted_iota(
            jnp.int32, (capacity, sensors), 0
        )
        return dot((slot == target).astype(F32).astype(BF16), values).astype(BF16)

    def row_copy(kind, offset):
        return pltpu.make_async_remote_copy(
            src_ref=send_rows.at[kind, offset],
            dst_ref=got_rows.at[kind, offset],
            send_sem=send_sem.at[kind, offset],
            recv_sem=got_sem.at[kind, offset],
            device_id={"grp": other_group(offset)},
            device_id_type=MESH,
        )

    for kind, values in enumerate((scaled, misfit)):
        ready = None
        for offset in group_order + [0]:
            send_rows[kind, offset] = place(values, offset)
            if ready is None and kind == 0:
                pl.semaphore_wait(barrier, groups + tiles - 2)
            if ready is not None:
                row_copy(kind, ready).start()
            ready = offset

    gram = (0, gram_part, gram_pieces, gram_mine, gram_whole)
    cross = (1, cross_part, cross_pieces, cross_mine, cross_out)

    def rows_of(mine, tile):
        rows = mine.shape[0]
        return pl.ds(pl.multiple_of(tile * rows, rows), rows)

    def piece_copy(one, offset):
        which, part, pieces, mine, _ = one
        return pltpu.make_async_remote_copy(
            src_ref=part.at[rows_of(mine, other_tile(offset))],
            dst_ref=pieces.at[offset],
            send_sem=piece_send.at[which, offset],
            recv_sem=piece_got.at[which, offset],
            device_id={"tile": other_tile(offset)},
            device_id_type=MESH,
        )

    def whole_copy(one, offset, owner):
        which, _, _, mine, whole = one
        return pltpu.make_async_remote_copy(
            src_ref=mine,
            dst_ref=whole.at[rows_of(mine, owner)],
            send_sem=whole_send.at[which, offset],
            recv_sem=whole_got.at[which, offset],
            device_id={"tile": other_tile(offset)},
            device_id_type=MESH,
        )

    def add_up(kind):
        total = dot_rows(send_rows[0, 0], send_rows[kind, 0])
        for offset in group_order:
            row_copy(kind, offset).wait_recv()
            total = total + dot_rows(got_rows[0, offset], got_rows[kind, offset])
        return total

    def send_pieces(one):
        for offset in tile_order:
            piece_copy(one, offset).start()

    def spread(one):
        _, part, pieces, mine, whole = one
        total = part[rows_of(mine, my_tile)]
        for offset in tile_order[::-1]:
            piece_copy(one, offset).wait_recv()
            total = total + pieces[offset]
        mine[...] = total
        whole[rows_of(mine, my_tile)] = total
        for offset in tile_order:
            whole_copy(one, offset, my_tile).start()

    def finish(one):
        for offset in tile_order[::-1]:
            whole_copy(one, offset, other_tile(offset, -1)).wait_recv()

    total = add_up(0)
    gram_part[0:half] = total[:half, :half]
    gram_part[half : 2 * half] = total[:half, half:]
    gram_part[2 * half :] = total[half:, half:]
    send_pieces(gram)
    spread(gram)
    cross_part[...] = add_up(1)
    send_pieces(cross)

    finish(gram)
    gram_out[:half, :half] = gram_whole[0:half]
    gram_out[:half, half:] = gram_whole[half : 2 * half]
    gram_out[half:, :half] = gram_whole[half : 2 * half].T
    gram_out[half:, half:] = gram_whole[2 * half :]

    identity = (
        lax.broadcasted_iota(jnp.int32, (members, members), 0)
        == lax.broadcasted_iota(jnp.int32, (members, members), 1)
    ).astype(F32)
    matrix = gram_out[...] + identity
    bound = jnp.max(jnp.sum(jnp.abs(matrix), axis=1, keepdims=True), axis=0, keepdims=True)
    bound_out[...] = jnp.broadcast_to(bound, bound_out.shape)

    low_end, high_end = jnp.ones_like(bound), bound
    for step in range(STEPS):
        scale = 2.0 / (low_end + high_end)
        low_end = scale * low_end * (2.0 - scale * low_end)
        high_end = jnp.ones_like(bound)
        if step == 0:
            factor = 2.0 * scale * identity - (scale * scale) * matrix
            pair[:members] = factor
            high, low = split(factor)
            pair[members:] = dot_split(matrix, high, low)
        else:
            factor = 2.0 * scale * identity - (scale * scale) * pair[members:]
            high, low = split(factor)
            if step == STEPS - 1:
                inverse_out[...] = dot_split(pair[:members], high, low)
            else:
                pair[...] = dot_split(pair[...], high, low)
        if step == STEPS // 2:
            spread(cross)

    finish(cross)
    for kind in range(2):
        for offset in group_order:
            row_copy(kind, offset).wait_send()
    for one in (gram, cross):
        for offset in tile_order:
            piece_copy(one, offset).wait_send()
            whole_copy(one, offset, my_tile).wait_send()


def sums(groups, tiles, position, bucket, sigma, field, observed):
    cells, members = field.shape
    sensors = position.shape[1]
    capacity = sensors // 4
    half = members // 2
    square = jax.ShapeDtypeStruct((members, members), F32)
    inputs = (position, bucket, sigma, field, observed)
    return pl.pallas_call(
        functools.partial(exchange, groups, tiles),
        out_shape=[square, square, square, jax.ShapeDtypeStruct((8, 128), F32)],
        in_specs=[HBM] * 5,
        out_specs=[VMEM] * 4,
        scratch_shapes=[
            pltpu.VMEM((1, sensors), jnp.int32),
            pltpu.VMEM((1, sensors), jnp.int32),
            pltpu.VMEM((1, sensors), F32),
            pltpu.VMEM((sensors, members), BF16),
            pltpu.VMEM((cells, members), BF16),
            pltpu.VMEM((sensors, members), F32),
            pltpu.VMEM((2, groups, capacity, members), BF16),
            pltpu.VMEM((2, groups, capacity, members), BF16),
            pltpu.VMEM((3 * half, half), F32),
            pltpu.VMEM((tiles, 3 * half // tiles, half), F32),
            pltpu.VMEM((3 * half // tiles, half), F32),
            pltpu.VMEM((3 * half, half), F32),
            pltpu.VMEM((members, members), F32),
            pltpu.VMEM((tiles, members // tiles, members), F32),
            pltpu.VMEM((members // tiles, members), F32),
            pltpu.VMEM((2 * members, members), F32),
            pltpu.SemaphoreType.DMA((4,)),
            pltpu.SemaphoreType.DMA((cells // BLOCK,)),
            pltpu.SemaphoreType.DMA((2, groups)),
            pltpu.SemaphoreType.DMA((2, groups)),
            pltpu.SemaphoreType.DMA((2, tiles)),
            pltpu.SemaphoreType.DMA((2, tiles)),
            pltpu.SemaphoreType.DMA((2, tiles)),
            pltpu.SemaphoreType.DMA((2, tiles)),
        ],
        compiler_params=pltpu.CompilerParams(
            collective_id=0, has_side_effects=True, vmem_limit_bytes=24 << 20
        ),
        cost_estimate=pl.CostEstimate(
            flops=4 << 30, bytes_accessed=100 << 20, transcendentals=0
        ),
        name="sums",
    )(*(pltpu.with_memory_space_constraint(x, pltpu.HBM) for x in inputs))


def apply(ready, gram, cross, bound, values, out, stored, inverse, transform, store_sem):
    total_rows, members = values.shape
    steps = total_rows // ROW_TILE
    safe = bound[0, 0] <= SAFE_BOUND

    def finish(matrix):
        high, low = split(cross[...])
        weights = dot_split(matrix, high, low)
        transform[...] = (weights / math.sqrt(members - 1)).astype(BF16)

    @pl.when(safe)
    def _():
        finish(ready[...])

    @pl.when(jnp.logical_not(safe))
    def _():
        down = lax.broadcasted_iota(jnp.int32, (members, members), 0)
        along = lax.broadcasted_iota(jnp.int32, (members, members), 1)
        inverse[...] = gram[...] + (down == along).astype(F32)
        line = lax.broadcasted_iota(jnp.int32, (members, 1), 0)
        spot = lax.broadcasted_iota(jnp.int32, (1, members), 1)

        def eliminate(step, _):
            now = inverse[...]
            here, there = (line == step), (spot == step)
            row = jnp.sum(jnp.where(here, now, 0.0), axis=0, keepdims=True)
            column = jnp.sum(jnp.where(there, now, 0.0), axis=1, keepdims=True)
            pivot = jnp.sum(jnp.where(there, row, 0.0), axis=1, keepdims=True)
            row = jnp.where(there, 1.0, row) / pivot
            column = jnp.where(here, 0.0, column)
            base = jnp.where(there, 0.0, now)
            inverse[...] = jnp.where(here, row, base - column * row)
            return 0

        lax.fori_loop(0, members, eliminate, 0)
        finish(inverse[...])

    def store(step, slot):
        part = pl.ds(step * ROW_TILE, ROW_TILE)
        return pltpu.make_async_copy(stored.at[slot], out.at[part], store_sem.at[slot])

    for step in range(steps):
        slot = step % 2
        now = values[pl.ds(step * ROW_TILE, ROW_TILE), :].astype(F32)
        anomaly = (now - jnp.mean(now, axis=1, keepdims=True)).astype(BF16)
        change = dot(anomaly, transform[...])
        if step >= 2:
            store(step - 2, slot).wait()
        stored[slot] = (now + change).astype(BF16)
        store(step, slot).start()
    for step in range(steps - 2, steps):
        store(step, step % 2).wait()


def update(inverse, gram, cross, bound, values):
    total_rows, members = values.shape
    return pl.pallas_call(
        apply,
        out_shape=jax.ShapeDtypeStruct(values.shape, values.dtype),
        in_specs=[VMEM] * 5,
        out_specs=HBM,
        scratch_shapes=[
            pltpu.VMEM((2, ROW_TILE, members), BF16),
            pltpu.VMEM((members, members), F32),
            pltpu.VMEM((members, members), BF16),
            pltpu.SemaphoreType.DMA((2,)),
        ],
        compiler_params=pltpu.CompilerParams(vmem_limit_bytes=32 << 20),
        name="update",
    )(inverse, gram, cross, bound, values)


def solution(mesh):
    groups, tiles = mesh.shape["grp"], mesh.shape["tile"]

    def shards(coefficients, field, position, bucket, sigma, observed):
        sensors = position.shape[0]
        solved = sums(
            groups,
            tiles,
            position.reshape(1, sensors),
            bucket.reshape(1, sensors),
            sigma.reshape(1, sensors),
            field,
            observed,
        )
        return update(*solved, coefficients)

    rows, flat = P(("grp", "tile"), None), P(("grp", "tile"))
    return jax.shard_map(
        shards,
        mesh=mesh,
        in_specs=(rows, rows, flat, rows, flat, rows),
        out_specs=rows,
        check_vma=False,
    )
```

```python
import functools
import math

import jax
import jax.numpy as jnp
from jax import lax
from jax.experimental import pallas as pl
from jax.experimental.pallas import tpu as pltpu
from jax.sharding import PartitionSpec as P

F32, BF16 = jnp.float32, jnp.bfloat16
MESH = pl.DeviceIdType.MESH
VMEM = pl.BlockSpec(memory_space=pltpu.VMEM)
HBM = pl.BlockSpec(memory_space=pltpu.HBM)
BLOCK = 512
SAFE_BOUND = 512.0
STEPS = 8
ROW_TILE = 2048
STORE_TILE = 1024


def dot(a, b):
    return lax.dot_general(a, b, (((1,), (0,)), ((), ())), preferred_element_type=F32)


def dot_rows(a, b):
    return lax.dot_general(a, b, (((0,), (0,)), ((), ())), preferred_element_type=F32)


def split(a):
    high = a.astype(BF16)
    return high, (a - high.astype(F32)).astype(BF16)


def dot_split(a, b_high, b_low):
    a_high, a_low = split(a)
    return dot(a_high, b_high) + (dot(a_low, b_high) + dot(a_high, b_low))


def exchange(
    groups,
    tiles,
    position,
    bucket,
    sigma,
    field,
    observed,
    coefficients,
    inverse_out,
    gram_out,
    cross_out,
    bound_out,
    values_out,
    anomaly_out,
    position_vmem,
    bucket_vmem,
    sigma_vmem,
    observed_vmem,
    field_vmem,
    picked,
    send_rows,
    got_rows,
    gram_part,
    gram_pieces,
    gram_mine,
    gram_whole,
    cross_part,
    cross_pieces,
    cross_mine,
    pair,
    small_sem,
    field_sem,
    value_sem,
    send_sem,
    got_sem,
    piece_send,
    piece_got,
    whole_send,
    whole_got,
):
    cells, members = field.shape
    sensors = position.shape[1]
    capacity = sensors // 4
    half = members // 2
    root_scale = math.sqrt(members - 1)
    my_group, my_tile = lax.axis_index("grp"), lax.axis_index("tile")
    ys, side = groups // 2, math.isqrt(tiles)

    def other_group(offset):
        far, core = offset // 2, offset % 2
        there = lax.rem(my_group // 2 + far, ys)
        return there * 2 + lax.rem(my_group + core, 2)

    def other_tile(offset, sign=1):
        far, near = offset // side, offset % side
        far, near = (far, near) if sign > 0 else (side - far, side - near)
        z = lax.rem(my_tile // side + far, side)
        return z * side + lax.rem(lax.rem(my_tile, side) + near, side)

    def ring(step, size):
        return min(step, size - step)

    tile_order = sorted(
        range(1, tiles), key=lambda o: -ring(o // side, side) - ring(o % side, side)
    )
    group_order = sorted(range(1, groups), key=lambda o: -ring(o // 2, ys))

    small = [
        pltpu.make_async_copy(source, landing, small_sem.at[number])
        for number, (source, landing) in enumerate(
            (
                (position, position_vmem),
                (bucket, bucket_vmem),
                (sigma, sigma_vmem),
                (observed, observed_vmem),
            )
        )
    ]
    for copy in small[:3]:
        copy.start()
    loads = []
    for block in range(cells // BLOCK):
        part_rows = pl.ds(block * BLOCK, BLOCK)
        loads.append(
            pltpu.make_async_copy(field.at[part_rows], field_vmem.at[part_rows], field_sem.at[block])
        )
        loads[-1].start()
    small[3].start()

    def value_load(step):
        part_rows = pl.ds(pl.multiple_of(step * ROW_TILE, ROW_TILE), ROW_TILE)
        return pltpu.make_async_copy(
            coefficients.at[part_rows], values_out.at[part_rows], value_sem.at[step]
        )

    value_steps = coefficients.shape[0] // ROW_TILE

    barrier = pltpu.get_barrier_semaphore()
    for offset in group_order:
        pl.semaphore_signal(
            barrier, inc=1, device_id={"grp": other_group(offset)}, device_id_type=MESH
        )
    for offset in tile_order:
        pl.semaphore_signal(
            barrier, inc=1, device_id={"tile": other_tile(offset)}, device_id_type=MESH
        )

    for copy in small[:3]:
        copy.wait()
    cell = position_vmem[...]
    group = bucket_vmem[...]
    facts = jnp.concatenate(
        [cell.astype(F32), sigma_vmem[...], jnp.zeros((6, sensors), F32)], axis=0
    ).T
    cell_column, sigma_column = facts[:, 0:1].astype(jnp.int32), facts[:, 1:2]

    lane = lax.broadcasted_iota(jnp.int32, (sensors, sensors), 1)
    row = lax.broadcasted_iota(jnp.int32, (sensors, sensors), 0)
    earlier = (row < lane).astype(F32).astype(BF16)
    member_of = (lax.broadcasted_iota(jnp.int32, (groups, sensors), 0) == group).astype(F32)
    before = dot(member_of.astype(BF16), earlier)
    rank = jnp.sum(before * member_of, axis=0, keepdims=True).astype(jnp.int32)
    target = group * capacity + rank

    for block in range(cells // BLOCK):
        part_rows = pl.ds(block * BLOCK, BLOCK)
        chosen = (
            lax.broadcasted_iota(jnp.int32, (sensors, BLOCK), 1) == cell_column - block * BLOCK
        )
        loads[block].wait()
        value = dot(chosen.astype(F32).astype(BF16), field_vmem[part_rows, :])
        if block == 0:
            picked[...] = value
        else:
            picked[...] += value

    kept = picked[...]
    mean = jnp.mean(kept, axis=1, keepdims=True)
    scaled = ((kept - mean) / (sigma_column * root_scale)).astype(BF16)
    small[3].wait()
    misfit = ((observed_vmem[...].astype(F32) - kept) / sigma_column).astype(BF16)

    def place(values, offset):
        slot = other_group(offset) * capacity + lax.broadcasted_iota(
            jnp.int32, (capacity, sensors), 0
        )
        return dot((slot == target).astype(F32).astype(BF16), values).astype(BF16)

    def row_copy(kind, offset):
        return pltpu.make_async_remote_copy(
            src_ref=send_rows.at[kind, offset],
            dst_ref=got_rows.at[kind, offset],
            send_sem=send_sem.at[kind, offset],
            recv_sem=got_sem.at[kind, offset],
            device_id={"grp": other_group(offset)},
            device_id_type=MESH,
        )

    for kind, values in enumerate((scaled, misfit)):
        ready = None
        for offset in group_order + [0]:
            send_rows[kind, offset] = place(values, offset)
            if ready is None and kind == 0:
                pl.semaphore_wait(barrier, groups + tiles - 2)
            if ready is not None:
                row_copy(kind, ready).start()
            ready = offset

    def center(step, _):
        value_load(step).wait()
        part_rows = pl.ds(pl.multiple_of(step * ROW_TILE, ROW_TILE), ROW_TILE)
        now = values_out[part_rows, :].astype(F32)
        anomaly_out[part_rows, :] = (now - jnp.mean(now, axis=1, keepdims=True)).astype(BF16)
        return 0

    for step in range(value_steps):
        value_load(step).start()
    lax.fori_loop(0, value_steps, center, 0)

    gram = (0, gram_part, gram_pieces, gram_mine, gram_whole)
    cross = (1, cross_part, cross_pieces, cross_mine, cross_out)

    def rows_of(mine, tile):
        rows = mine.shape[0]
        return pl.ds(pl.multiple_of(tile * rows, rows), rows)

    def piece_copy(one, offset):
        which, part, pieces, mine, _ = one
        return pltpu.make_async_remote_copy(
            src_ref=part.at[rows_of(mine, other_tile(offset))],
            dst_ref=pieces.at[offset],
            send_sem=piece_send.at[which, offset],
            recv_sem=piece_got.at[which, offset],
            device_id={"tile": other_tile(offset)},
            device_id_type=MESH,
        )

    def whole_copy(one, offset, owner):
        which, _, _, mine, whole = one
        return pltpu.make_async_remote_copy(
            src_ref=mine,
            dst_ref=whole.at[rows_of(mine, owner)],
            send_sem=whole_send.at[which, offset],
            recv_sem=whole_got.at[which, offset],
            device_id={"tile": other_tile(offset)},
            device_id_type=MESH,
        )

    def add_up(kind):
        total = dot_rows(send_rows[0, 0], send_rows[kind, 0])
        for offset in group_order:
            row_copy(kind, offset).wait_recv()
            total = total + dot_rows(got_rows[0, offset], got_rows[kind, offset])
        return total

    def send_pieces(one):
        for offset in tile_order:
            piece_copy(one, offset).start()

    def spread(one):
        _, part, pieces, mine, whole = one
        total = part[rows_of(mine, my_tile)]
        for offset in tile_order[::-1]:
            piece_copy(one, offset).wait_recv()
            total = total + pieces[offset]
        mine[...] = total
        whole[rows_of(mine, my_tile)] = total
        for offset in tile_order:
            whole_copy(one, offset, my_tile).start()

    def finish(one):
        for offset in tile_order[::-1]:
            whole_copy(one, offset, other_tile(offset, -1)).wait_recv()

    total = add_up(0)
    gram_part[0:half] = total[:half, :half]
    gram_part[half : 2 * half] = total[:half, half:]
    gram_part[2 * half :] = total[half:, half:]
    send_pieces(gram)
    spread(gram)
    cross_part[...] = add_up(1)
    send_pieces(cross)

    finish(gram)
    gram_out[:half, :half] = gram_whole[0:half]
    gram_out[:half, half:] = gram_whole[half : 2 * half]
    gram_out[half:, :half] = gram_whole[half : 2 * half].T
    gram_out[half:, half:] = gram_whole[2 * half :]

    identity = (
        lax.broadcasted_iota(jnp.int32, (members, members), 0)
        == lax.broadcasted_iota(jnp.int32, (members, members), 1)
    ).astype(F32)
    matrix = gram_out[...] + identity
    bound = jnp.max(jnp.sum(jnp.abs(matrix), axis=1, keepdims=True), axis=0, keepdims=True)
    bound_out[...] = jnp.broadcast_to(bound, bound_out.shape)

    low_end, high_end = jnp.ones_like(bound), bound
    for step in range(STEPS):
        scale = 2.0 / (low_end + high_end)
        low_end = scale * low_end * (2.0 - scale * low_end)
        high_end = jnp.ones_like(bound)
        if step == 0:
            factor = 2.0 * scale * identity - (scale * scale) * matrix
            pair[:members] = factor
            high, low = split(factor)
            pair[members:] = dot_split(matrix, high, low)
        else:
            factor = 2.0 * scale * identity - (scale * scale) * pair[members:]
            high, low = split(factor)
            if step == STEPS - 1:
                inverse_out[...] = dot_split(pair[:members], high, low)
            else:
                pair[...] = dot_split(pair[...], high, low)
        if step == STEPS // 2:
            spread(cross)

    finish(cross)
    for kind in range(2):
        for offset in group_order:
            row_copy(kind, offset).wait_send()
    for one in (gram, cross):
        for offset in tile_order:
            piece_copy(one, offset).wait_send()
            whole_copy(one, offset, my_tile).wait_send()


def sums(groups, tiles, position, bucket, sigma, field, observed, coefficients):
    cells, members = field.shape
    sensors = position.shape[1]
    capacity = sensors // 4
    half = members // 2
    square = jax.ShapeDtypeStruct((members, members), F32)
    ensemble = jax.ShapeDtypeStruct(coefficients.shape, coefficients.dtype)
    inputs = (position, bucket, sigma, field, observed, coefficients)
    return pl.pallas_call(
        functools.partial(exchange, groups, tiles),
        out_shape=[square, square, square, jax.ShapeDtypeStruct((8, 128), F32)]
        + [ensemble] * 2,
        in_specs=[HBM] * 6,
        out_specs=[VMEM] * 6,
        scratch_shapes=[
            pltpu.VMEM((1, sensors), jnp.int32),
            pltpu.VMEM((1, sensors), jnp.int32),
            pltpu.VMEM((1, sensors), F32),
            pltpu.VMEM((sensors, members), BF16),
            pltpu.VMEM((cells, members), BF16),
            pltpu.VMEM((sensors, members), F32),
            pltpu.VMEM((2, groups, capacity, members), BF16),
            pltpu.VMEM((2, groups, capacity, members), BF16),
            pltpu.VMEM((3 * half, half), F32),
            pltpu.VMEM((tiles, 3 * half // tiles, half), F32),
            pltpu.VMEM((3 * half // tiles, half), F32),
            pltpu.VMEM((3 * half, half), F32),
            pltpu.VMEM((members, members), F32),
            pltpu.VMEM((tiles, members // tiles, members), F32),
            pltpu.VMEM((members // tiles, members), F32),
            pltpu.VMEM((2 * members, members), F32),
            pltpu.SemaphoreType.DMA((4,)),
            pltpu.SemaphoreType.DMA((cells // BLOCK,)),
            pltpu.SemaphoreType.DMA((coefficients.shape[0] // ROW_TILE,)),
            pltpu.SemaphoreType.DMA((2, groups)),
            pltpu.SemaphoreType.DMA((2, groups)),
            pltpu.SemaphoreType.DMA((2, tiles)),
            pltpu.SemaphoreType.DMA((2, tiles)),
            pltpu.SemaphoreType.DMA((2, tiles)),
            pltpu.SemaphoreType.DMA((2, tiles)),
        ],
        compiler_params=pltpu.CompilerParams(
            collective_id=0, has_side_effects=True, vmem_limit_bytes=16 << 20
        ),
        cost_estimate=pl.CostEstimate(
            flops=4 << 30, bytes_accessed=100 << 20, transcendentals=0
        ),
        name="sums",
    )(*(pltpu.with_memory_space_constraint(x, pltpu.HBM) for x in inputs))


def apply(ready, gram, cross, bound, values, anomaly, out, stored, inverse, transform, store_sem):
    total_rows, members = values.shape
    steps = total_rows // STORE_TILE
    safe = bound[0, 0] <= SAFE_BOUND

    def finish(matrix):
        high, low = split(cross[...])
        weights = dot_split(matrix, high, low)
        transform[...] = (weights / math.sqrt(members - 1)).astype(BF16)

    @pl.when(safe)
    def _():
        finish(ready[...])

    @pl.when(jnp.logical_not(safe))
    def _():
        down = lax.broadcasted_iota(jnp.int32, (members, members), 0)
        along = lax.broadcasted_iota(jnp.int32, (members, members), 1)
        inverse[...] = gram[...] + (down == along).astype(F32)
        line = lax.broadcasted_iota(jnp.int32, (members, 1), 0)
        spot = lax.broadcasted_iota(jnp.int32, (1, members), 1)

        def eliminate(step, _):
            now = inverse[...]
            here, there = (line == step), (spot == step)
            row = jnp.sum(jnp.where(here, now, 0.0), axis=0, keepdims=True)
            column = jnp.sum(jnp.where(there, now, 0.0), axis=1, keepdims=True)
            pivot = jnp.sum(jnp.where(there, row, 0.0), axis=1, keepdims=True)
            row = jnp.where(there, 1.0, row) / pivot
            column = jnp.where(here, 0.0, column)
            base = jnp.where(there, 0.0, now)
            inverse[...] = jnp.where(here, row, base - column * row)
            return 0

        lax.fori_loop(0, members, eliminate, 0)
        finish(inverse[...])

    def store(step):
        rows = pl.ds(step * STORE_TILE, STORE_TILE)
        return pltpu.make_async_copy(stored.at[rows], out.at[rows], store_sem.at[step])

    for step in range(steps):
        rows = pl.ds(step * STORE_TILE, STORE_TILE)
        change = dot(anomaly[rows, :], transform[...])
        stored[rows, :] = (values[rows, :].astype(F32) + change).astype(BF16)
        store(step).start()
    for step in range(steps):
        store(step).wait()


def update(inverse, gram, cross, bound, values, anomaly):
    total_rows, members = values.shape
    return pl.pallas_call(
        apply,
        out_shape=jax.ShapeDtypeStruct(values.shape, values.dtype),
        in_specs=[VMEM] * 6,
        out_specs=HBM,
        scratch_shapes=[
            pltpu.VMEM((total_rows, members), BF16),
            pltpu.VMEM((members, members), F32),
            pltpu.VMEM((members, members), BF16),
            pltpu.SemaphoreType.DMA((total_rows // STORE_TILE,)),
        ],
        compiler_params=pltpu.CompilerParams(vmem_limit_bytes=16 << 20),
        name="update",
    )(inverse, gram, cross, bound, values, anomaly)


def solution(mesh):
    groups, tiles = mesh.shape["grp"], mesh.shape["tile"]

    def shards(coefficients, field, position, bucket, sigma, observed):
        sensors = position.shape[0]
        solved = sums(
            groups,
            tiles,
            position.reshape(1, sensors),
            bucket.reshape(1, sensors),
            sigma.reshape(1, sensors),
            field,
            observed,
            coefficients,
        )
        return update(*solved)

    rows, flat = P(("grp", "tile"), None), P(("grp", "tile"))
    return jax.shard_map(
        shards,
        mesh=mesh,
        in_specs=(rows, rows, flat, rows, flat, rows),
        out_specs=rows,
        check_vma=False,
    )
```

```python
import functools
import math

import jax
import jax.numpy as jnp
from jax import lax
from jax.experimental import pallas as pl
from jax.experimental.pallas import tpu as pltpu
from jax.sharding import PartitionSpec as P

F32, BF16 = jnp.float32, jnp.bfloat16
MESH = pl.DeviceIdType.MESH
VMEM = pl.BlockSpec(memory_space=pltpu.VMEM)
HBM = pl.BlockSpec(memory_space=pltpu.HBM)
BLOCK = 2048
LANES = 128
SAFE_BOUND = 512.0
STEPS = 8
ROW_TILE = 2048
STORE_TILE = 1024


def dot(a, b):
    return lax.dot_general(a, b, (((1,), (0,)), ((), ())), preferred_element_type=F32)


def dot_rows(a, b):
    return lax.dot_general(a, b, (((0,), (0,)), ((), ())), preferred_element_type=F32)


def split(a):
    high = a.astype(BF16)
    return high, (a - high.astype(F32)).astype(BF16)


def dot_split(a, b_high, b_low):
    a_high, a_low = split(a)
    return dot(a_high, b_high) + (dot(a_low, b_high) + dot(a_high, b_low))


def exchange(
    groups,
    tiles,
    position,
    bucket,
    sigma,
    field,
    observed,
    coefficients,
    inverse_out,
    gram_out,
    cross_out,
    bound_out,
    values_out,
    anomaly_out,
    position_vmem,
    bucket_vmem,
    sigma_vmem,
    observed_vmem,
    field_vmem,
    picked,
    send_rows,
    got_rows,
    send_half,
    got_half,
    gram_part,
    gram_pieces,
    gram_mine,
    gram_whole,
    cross_part,
    cross_pieces,
    cross_mine,
    cross_whole,
    pair,
    small_sem,
    field_sem,
    value_sem,
    send_sem,
    got_sem,
    piece_send,
    piece_got,
    whole_send,
    whole_got,
):
    cells, members = field.shape
    sensors = position.shape[1]
    capacity = sensors // 4
    half = members // 2
    root_scale = math.sqrt(members - 1)
    my_group, my_tile = lax.axis_index("grp"), lax.axis_index("tile")
    ys, side = groups // 2, math.isqrt(tiles)

    def other_group(offset):
        far, core = offset // 2, offset % 2
        there = lax.rem(my_group // 2 + far, ys)
        return there * 2 + lax.rem(my_group + core, 2)

    def other_tile(offset, sign=1):
        far, near = offset // side, offset % side
        far, near = (far, near) if sign > 0 else (side - far, side - near)
        z = lax.rem(my_tile // side + far, side)
        return z * side + lax.rem(lax.rem(my_tile, side) + near, side)

    def ring(step, size):
        return min(step, size - step)

    tile_order = sorted(
        range(1, tiles), key=lambda o: -ring(o // side, side) - ring(o % side, side)
    )
    group_order = sorted(range(1, groups), key=lambda o: -ring(o // 2, ys))

    small = [
        pltpu.make_async_copy(source, landing, small_sem.at[number])
        for number, (source, landing) in enumerate(
            (
                (position, position_vmem),
                (bucket, bucket_vmem),
                (sigma, sigma_vmem),
                (observed, observed_vmem),
            )
        )
    ]
    for copy in small[:3]:
        copy.start()
    loads = []
    for block in range(cells // BLOCK):
        part_rows = pl.ds(block * BLOCK, BLOCK)
        loads.append(
            pltpu.make_async_copy(field.at[part_rows], field_vmem.at[part_rows], field_sem.at[block])
        )
        loads[-1].start()
    small[3].start()

    def value_load(step):
        part_rows = pl.ds(pl.multiple_of(step * ROW_TILE, ROW_TILE), ROW_TILE)
        return pltpu.make_async_copy(
            coefficients.at[part_rows], values_out.at[part_rows], value_sem.at[step]
        )

    value_steps = coefficients.shape[0] // ROW_TILE

    barrier = pltpu.get_barrier_semaphore()
    for offset in group_order:
        pl.semaphore_signal(
            barrier, inc=1, device_id={"grp": other_group(offset)}, device_id_type=MESH
        )
    for offset in tile_order:
        pl.semaphore_signal(
            barrier, inc=1, device_id={"tile": other_tile(offset)}, device_id_type=MESH
        )

    lane = lax.broadcasted_iota(jnp.int32, (sensors, sensors), 1)
    row = lax.broadcasted_iota(jnp.int32, (sensors, sensors), 0)
    earlier = (row < lane).astype(F32).astype(BF16)
    for copy in small[:3]:
        copy.wait()
    cell = position_vmem[...].astype(F32)
    block_of = jnp.floor(cell * (1.0 / LANES))
    inverse_sigma = 1.0 / sigma_vmem[...]
    facts = jnp.concatenate(
        [
            block_of,
            cell - block_of * LANES,
            inverse_sigma,
            inverse_sigma * (1.0 / root_scale),
            jnp.zeros((4, sensors), F32),
        ],
        axis=0,
    ).T
    block_column = jnp.broadcast_to(facts[:, 0:1], (sensors, LANES)).astype(BF16)
    spots = lax.broadcasted_iota(jnp.int32, (sensors, LANES), 1).astype(F32)
    spot_hit = (spots == facts[:, 1:2]).astype(F32).astype(BF16)
    none = jnp.zeros_like(spot_hit)

    value = None
    for block in range(cells // BLOCK):
        chosen = jnp.concatenate(
            [
                jnp.where(block_column == float(block * (BLOCK // LANES) + k), spot_hit, none)
                for k in range(BLOCK // LANES)
            ],
            axis=1,
        )
        loads[block].wait()
        more = dot(chosen, field_vmem[pl.ds(block * BLOCK, BLOCK), :])
        value = more if value is None else value + more
    picked[...] = value

    group = bucket_vmem[...]
    member_of = (lax.broadcasted_iota(jnp.int32, (groups, sensors), 0) == group).astype(F32)
    before = dot(member_of.astype(BF16), earlier)
    rank = jnp.sum(before * member_of, axis=0, keepdims=True)
    target = group.astype(F32) * capacity + rank

    kept = picked[...]
    mean = jnp.mean(kept, axis=1, keepdims=True)
    scaled = ((kept - mean) * facts[:, 3:4]).astype(BF16)
    small[3].wait()
    misfit = ((observed_vmem[...].astype(F32) - kept) * facts[:, 2:3]).astype(BF16)

    slots = lax.broadcasted_iota(jnp.int32, (capacity, sensors), 0).astype(F32).astype(BF16)

    def place(values, offset):
        first = (other_group(offset) * capacity).astype(F32)
        local = jnp.clip(target - first, -1.0, float(capacity)).astype(BF16)
        hit = jnp.where(slots == local, jnp.ones_like(slots), jnp.zeros_like(slots))
        return dot(hit, values).astype(BF16)

    def row_copy(kind, offset):
        source, landing = send_rows.at[offset], got_rows.at[offset]
        if kind:
            source, landing = send_half.at[kind - 1, offset], got_half.at[kind - 1, offset]
        return pltpu.make_async_remote_copy(
            src_ref=source,
            dst_ref=landing,
            send_sem=send_sem.at[kind, offset],
            recv_sem=got_sem.at[kind, offset],
            device_id={"grp": other_group(offset)},
            device_id_type=MESH,
        )

    ready = None
    for offset in group_order + [0]:
        send_rows[offset] = place(scaled, offset)
        if ready is None:
            pl.semaphore_wait(barrier, groups + tiles - 2)
        else:
            row_copy(0, ready).start()
        ready = offset
    ready = None
    for offset in group_order + [0]:
        placed = place(misfit, offset)
        send_half[0, offset] = placed[:, :half]
        send_half[1, offset] = placed[:, half:]
        if ready is not None:
            row_copy(1, ready).start()
        ready = offset
    for offset in group_order:
        row_copy(2, offset).start()

    def center(step, _):
        value_load(step).wait()
        part_rows = pl.ds(pl.multiple_of(step * ROW_TILE, ROW_TILE), ROW_TILE)
        now = values_out[part_rows, :].astype(F32)
        anomaly_out[part_rows, :] = (now - jnp.mean(now, axis=1, keepdims=True)).astype(BF16)
        return 0

    for step in range(value_steps):
        value_load(step).start()
    lax.fori_loop(0, value_steps, center, 0)

    gram = (0, gram_part, gram_pieces, gram_mine, gram_whole)
    crosses = [
        (
            1 + side_half,
            cross_part.at[side_half],
            cross_pieces.at[side_half],
            cross_mine.at[side_half],
            cross_whole.at[side_half],
        )
        for side_half in range(2)
    ]

    def rows_of(mine, tile):
        rows = mine.shape[0]
        return pl.ds(pl.multiple_of(tile * rows, rows), rows)

    def piece_copy(one, offset):
        which, part, pieces, mine, _ = one
        return pltpu.make_async_remote_copy(
            src_ref=part.at[rows_of(mine, other_tile(offset))],
            dst_ref=pieces.at[offset],
            send_sem=piece_send.at[which, offset],
            recv_sem=piece_got.at[which, offset],
            device_id={"tile": other_tile(offset)},
            device_id_type=MESH,
        )

    def whole_copy(one, offset, owner):
        which, _, _, mine, whole = one
        return pltpu.make_async_remote_copy(
            src_ref=mine,
            dst_ref=whole.at[rows_of(mine, owner)],
            send_sem=whole_send.at[which, offset],
            recv_sem=whole_got.at[which, offset],
            device_id={"tile": other_tile(offset)},
            device_id_type=MESH,
        )

    def add_up(kind):
        other = send_half.at[kind - 1] if kind else send_rows
        total = dot_rows(send_rows[0], other[0])
        other = got_half.at[kind - 1] if kind else got_rows
        for offset in group_order:
            row_copy(kind, offset).wait_recv()
            total = total + dot_rows(got_rows[offset], other[offset])
        return total

    def send_pieces(one):
        for offset in tile_order:
            piece_copy(one, offset).start()

    def spread(one):
        _, part, pieces, mine, whole = one
        total = part[rows_of(mine, my_tile)]
        for offset in tile_order[::-1]:
            piece_copy(one, offset).wait_recv()
            total = total + pieces[offset]
        mine[...] = total
        whole[rows_of(mine, my_tile)] = total
        for offset in tile_order:
            whole_copy(one, offset, my_tile).start()

    def finish(one):
        for offset in tile_order[::-1]:
            whole_copy(one, offset, other_tile(offset, -1)).wait_recv()

    total = add_up(0)
    gram_part[0:half] = total[:half, :half]
    gram_part[half : 2 * half] = total[:half, half:]
    gram_part[2 * half :] = total[half:, half:]
    send_pieces(gram)
    cross_part[0] = add_up(1)
    send_pieces(crosses[0])
    spread(gram)
    cross_part[1] = add_up(2)
    send_pieces(crosses[1])
    spread(crosses[0])

    finish(gram)
    spread(crosses[1])
    gram_out[:half, :half] = gram_whole[0:half]
    gram_out[:half, half:] = gram_whole[half : 2 * half]
    gram_out[half:, :half] = gram_whole[half : 2 * half].T
    gram_out[half:, half:] = gram_whole[2 * half :]

    identity = (
        lax.broadcasted_iota(jnp.int32, (members, members), 0)
        == lax.broadcasted_iota(jnp.int32, (members, members), 1)
    ).astype(F32)
    matrix = gram_out[...] + identity
    bound = jnp.max(jnp.sum(jnp.abs(matrix), axis=1, keepdims=True), axis=0, keepdims=True)
    bound_out[...] = jnp.broadcast_to(bound, bound_out.shape)

    low_end, high_end = jnp.ones_like(bound), bound
    for step in range(STEPS):
        scale = 2.0 / (low_end + high_end)
        low_end = scale * low_end * (2.0 - scale * low_end)
        high_end = jnp.ones_like(bound)
        if step == 0:
            factor = 2.0 * scale * identity - (scale * scale) * matrix
            pair[:members] = factor
            high, low = split(factor)
            pair[members:] = dot_split(matrix, high, low)
        else:
            factor = 2.0 * scale * identity - (scale * scale) * pair[members:]
            high, low = split(factor)
            if step == STEPS - 1:
                inverse_out[...] = dot_split(pair[:members], high, low)
            else:
                pair[...] = dot_split(pair[...], high, low)

    for side_half, one in enumerate(crosses):
        finish(one)
        cross_out[:, side_half * half : (side_half + 1) * half] = cross_whole[side_half]
    for kind in range(3):
        for offset in group_order:
            row_copy(kind, offset).wait_send()
    for one in [gram] + crosses:
        for offset in tile_order:
            piece_copy(one, offset).wait_send()
            whole_copy(one, offset, my_tile).wait_send()


def sums(groups, tiles, position, bucket, sigma, field, observed, coefficients):
    cells, members = field.shape
    sensors = position.shape[1]
    capacity = sensors // 4
    half = members // 2
    square = jax.ShapeDtypeStruct((members, members), F32)
    ensemble = jax.ShapeDtypeStruct(coefficients.shape, coefficients.dtype)
    inputs = (position, bucket, sigma, field, observed, coefficients)
    return pl.pallas_call(
        functools.partial(exchange, groups, tiles),
        out_shape=[square, square, square, jax.ShapeDtypeStruct((8, 128), F32)]
        + [ensemble] * 2,
        in_specs=[HBM] * 6,
        out_specs=[VMEM] * 6,
        scratch_shapes=[
            pltpu.VMEM((1, sensors), jnp.int32),
            pltpu.VMEM((1, sensors), jnp.int32),
            pltpu.VMEM((1, sensors), F32),
            pltpu.VMEM((sensors, members), BF16),
            pltpu.VMEM((cells, members), BF16),
            pltpu.VMEM((sensors, members), F32),
            pltpu.VMEM((groups, capacity, members), BF16),
            pltpu.VMEM((groups, capacity, members), BF16),
            pltpu.VMEM((2, groups, capacity, half), BF16),
            pltpu.VMEM((2, groups, capacity, half), BF16),
            pltpu.VMEM((3 * half, half), F32),
            pltpu.VMEM((tiles, 3 * half // tiles, half), F32),
            pltpu.VMEM((3 * half // tiles, half), F32),
            pltpu.VMEM((3 * half, half), F32),
            pltpu.VMEM((2, members, half), F32),
            pltpu.VMEM((2, tiles, members // tiles, half), F32),
            pltpu.VMEM((2, members // tiles, half), F32),
            pltpu.VMEM((2, members, half), F32),
            pltpu.VMEM((2 * members, members), F32),
            pltpu.SemaphoreType.DMA((4,)),
            pltpu.SemaphoreType.DMA((cells // BLOCK,)),
            pltpu.SemaphoreType.DMA((coefficients.shape[0] // ROW_TILE,)),
            pltpu.SemaphoreType.DMA((3, groups)),
            pltpu.SemaphoreType.DMA((3, groups)),
            pltpu.SemaphoreType.DMA((3, tiles)),
            pltpu.SemaphoreType.DMA((3, tiles)),
            pltpu.SemaphoreType.DMA((3, tiles)),
            pltpu.SemaphoreType.DMA((3, tiles)),
        ],
        compiler_params=pltpu.CompilerParams(
            collective_id=0, has_side_effects=True, vmem_limit_bytes=16 << 20
        ),
        cost_estimate=pl.CostEstimate(
            flops=4 << 30, bytes_accessed=100 << 20, transcendentals=0
        ),
        name="sums",
    )(*(pltpu.with_memory_space_constraint(x, pltpu.HBM) for x in inputs))


def apply(ready, gram, cross, bound, values, anomaly, out, stored, inverse, transform, store_sem):
    total_rows, members = values.shape
    steps = total_rows // STORE_TILE
    safe = bound[0, 0] <= SAFE_BOUND

    def finish(matrix):
        high, low = split(cross[...])
        weights = dot_split(matrix, high, low)
        transform[...] = (weights / math.sqrt(members - 1)).astype(BF16)

    @pl.when(safe)
    def _():
        finish(ready[...])

    @pl.when(jnp.logical_not(safe))
    def _():
        down = lax.broadcasted_iota(jnp.int32, (members, members), 0)
        along = lax.broadcasted_iota(jnp.int32, (members, members), 1)
        inverse[...] = gram[...] + (down == along).astype(F32)
        line = lax.broadcasted_iota(jnp.int32, (members, 1), 0)
        spot = lax.broadcasted_iota(jnp.int32, (1, members), 1)

        def eliminate(step, _):
            now = inverse[...]
            here, there = (line == step), (spot == step)
            row = jnp.sum(jnp.where(here, now, 0.0), axis=0, keepdims=True)
            column = jnp.sum(jnp.where(there, now, 0.0), axis=1, keepdims=True)
            pivot = jnp.sum(jnp.where(there, row, 0.0), axis=1, keepdims=True)
            row = jnp.where(there, 1.0, row) / pivot
            column = jnp.where(here, 0.0, column)
            base = jnp.where(there, 0.0, now)
            inverse[...] = jnp.where(here, row, base - column * row)
            return 0

        lax.fori_loop(0, members, eliminate, 0)
        finish(inverse[...])

    def store(step):
        rows = pl.ds(step * STORE_TILE, STORE_TILE)
        return pltpu.make_async_copy(stored.at[rows], out.at[rows], store_sem.at[step])

    for step in range(steps):
        rows = pl.ds(step * STORE_TILE, STORE_TILE)
        change = dot(anomaly[rows, :], transform[...])
        stored[rows, :] = (values[rows, :].astype(F32) + change).astype(BF16)
        store(step).start()
    for step in range(steps):
        store(step).wait()


def update(inverse, gram, cross, bound, values, anomaly):
    total_rows, members = values.shape
    return pl.pallas_call(
        apply,
        out_shape=jax.ShapeDtypeStruct(values.shape, values.dtype),
        in_specs=[VMEM] * 6,
        out_specs=HBM,
        scratch_shapes=[
            pltpu.VMEM((total_rows, members), BF16),
            pltpu.VMEM((members, members), F32),
            pltpu.VMEM((members, members), BF16),
            pltpu.SemaphoreType.DMA((total_rows // STORE_TILE,)),
        ],
        compiler_params=pltpu.CompilerParams(vmem_limit_bytes=16 << 20),
        name="update",
    )(inverse, gram, cross, bound, values, anomaly)


def solution(mesh):
    groups, tiles = mesh.shape["grp"], mesh.shape["tile"]

    def shards(coefficients, field, position, bucket, sigma, observed):
        sensors = position.shape[0]
        solved = sums(
            groups,
            tiles,
            position.reshape(1, sensors),
            bucket.reshape(1, sensors),
            sigma.reshape(1, sensors),
            field,
            observed,
            coefficients,
        )
        return update(*solved)

    rows, flat = P(("grp", "tile"), None), P(("grp", "tile"))
    return jax.shard_map(
        shards,
        mesh=mesh,
        in_specs=(rows, rows, flat, rows, flat, rows),
        out_specs=rows,
        check_vma=False,
    )
```

```python
import functools
import math

import jax
import jax.numpy as jnp
from jax import lax
from jax.experimental import pallas as pl
from jax.experimental.pallas import tpu as pltpu
from jax.sharding import PartitionSpec as P

F32, BF16 = jnp.float32, jnp.bfloat16
MESH = pl.DeviceIdType.MESH
VMEM = pl.BlockSpec(memory_space=pltpu.VMEM)
HBM = pl.BlockSpec(memory_space=pltpu.HBM)
BLOCK = 2048
LANES = 128
SAFE_BOUND = 256.0
STEPS = 7
ROW_TILE = 2048
STORE_TILE = 1024


def dot(a, b):
    return lax.dot_general(a, b, (((1,), (0,)), ((), ())), preferred_element_type=F32)


def dot_rows(a, b):
    return lax.dot_general(a, b, (((0,), (0,)), ((), ())), preferred_element_type=F32)


def split(a):
    high = a.astype(BF16)
    return high, (a - high.astype(F32)).astype(BF16)


def dot_split(a, b_high, b_low):
    a_high, a_low = split(a)
    return dot(a_high, b_high) + (dot(a_low, b_high) + dot(a_high, b_low))


def exchange(
    groups,
    tiles,
    position,
    bucket,
    sigma,
    field,
    observed,
    coefficients,
    inverse_out,
    gram_out,
    cross_out,
    bound_out,
    values_out,
    anomaly_out,
    position_vmem,
    bucket_vmem,
    sigma_vmem,
    observed_vmem,
    field_vmem,
    picked,
    send_rows,
    got_rows,
    send_half,
    got_half,
    gram_part,
    gram_pieces,
    gram_mine,
    gram_whole,
    cross_part,
    cross_pieces,
    cross_mine,
    cross_whole,
    pair,
    small_sem,
    field_sem,
    value_sem,
    send_sem,
    got_sem,
    piece_send,
    piece_got,
    whole_send,
    whole_got,
):
    cells, members = field.shape
    sensors = position.shape[1]
    capacity = sensors // 4
    half = members // 2
    root_scale = math.sqrt(members - 1)
    my_group, my_tile = lax.axis_index("grp"), lax.axis_index("tile")
    ys, side = groups // 2, math.isqrt(tiles)

    def other_group(offset):
        far, core = offset // 2, offset % 2
        there = lax.rem(my_group // 2 + far, ys)
        return there * 2 + lax.rem(my_group + core, 2)

    def other_tile(offset, sign=1):
        far, near = offset // side, offset % side
        far, near = (far, near) if sign > 0 else (side - far, side - near)
        z = lax.rem(my_tile // side + far, side)
        return z * side + lax.rem(lax.rem(my_tile, side) + near, side)

    def ring(step, size):
        return min(step, size - step)

    tile_order = sorted(
        range(1, tiles), key=lambda o: -ring(o // side, side) - ring(o % side, side)
    )
    group_order = sorted(range(1, groups), key=lambda o: -ring(o // 2, ys))

    small = [
        pltpu.make_async_copy(source, landing, small_sem.at[number])
        for number, (source, landing) in enumerate(
            (
                (position, position_vmem),
                (bucket, bucket_vmem),
                (sigma, sigma_vmem),
                (observed, observed_vmem),
            )
        )
    ]
    for copy in small[:3]:
        copy.start()
    loads = []
    for block in range(cells // BLOCK):
        part_rows = pl.ds(block * BLOCK, BLOCK)
        loads.append(
            pltpu.make_async_copy(field.at[part_rows], field_vmem.at[part_rows], field_sem.at[block])
        )
        loads[-1].start()
    small[3].start()

    def value_load(step):
        part_rows = pl.ds(pl.multiple_of(step * ROW_TILE, ROW_TILE), ROW_TILE)
        return pltpu.make_async_copy(
            coefficients.at[part_rows], values_out.at[part_rows], value_sem.at[step]
        )

    value_steps = coefficients.shape[0] // ROW_TILE

    barrier = pltpu.get_barrier_semaphore()
    for offset in group_order:
        pl.semaphore_signal(
            barrier, inc=1, device_id={"grp": other_group(offset)}, device_id_type=MESH
        )
    for offset in tile_order:
        pl.semaphore_signal(
            barrier, inc=1, device_id={"tile": other_tile(offset)}, device_id_type=MESH
        )

    lane = lax.broadcasted_iota(jnp.int32, (sensors, sensors), 1)
    row = lax.broadcasted_iota(jnp.int32, (sensors, sensors), 0)
    earlier = (row < lane).astype(F32).astype(BF16)
    for copy in small[:3]:
        copy.wait()
    cell = position_vmem[...].astype(F32)
    block_of = jnp.floor(cell * (1.0 / LANES))
    inverse_sigma = 1.0 / sigma_vmem[...]
    facts = jnp.concatenate(
        [
            block_of,
            cell - block_of * LANES,
            inverse_sigma,
            inverse_sigma * (1.0 / root_scale),
            jnp.zeros((4, sensors), F32),
        ],
        axis=0,
    ).T
    block_column = jnp.broadcast_to(facts[:, 0:1], (sensors, LANES)).astype(BF16)
    spots = lax.broadcasted_iota(jnp.int32, (sensors, LANES), 1).astype(F32)
    spot_hit = (spots == facts[:, 1:2]).astype(F32).astype(BF16)
    none = jnp.zeros_like(spot_hit)

    value = None
    for block in range(cells // BLOCK):
        chosen = jnp.concatenate(
            [
                jnp.where(block_column == float(block * (BLOCK // LANES) + k), spot_hit, none)
                for k in range(BLOCK // LANES)
            ],
            axis=1,
        )
        loads[block].wait()
        more = dot(chosen, field_vmem[pl.ds(block * BLOCK, BLOCK), :])
        value = more if value is None else value + more
    picked[...] = value

    group = bucket_vmem[...]
    member_of = (lax.broadcasted_iota(jnp.int32, (groups, sensors), 0) == group).astype(F32)
    before = dot(member_of.astype(BF16), earlier)
    rank = jnp.sum(before * member_of, axis=0, keepdims=True)
    target = group.astype(F32) * capacity + rank

    kept = picked[...]
    mean = jnp.mean(kept, axis=1, keepdims=True)
    scaled = ((kept - mean) * facts[:, 3:4]).astype(BF16)
    small[3].wait()
    misfit = ((observed_vmem[...].astype(F32) - kept) * facts[:, 2:3]).astype(BF16)

    slots = lax.broadcasted_iota(jnp.int32, (capacity, sensors), 0).astype(F32).astype(BF16)

    def place(values, offset):
        first = (other_group(offset) * capacity).astype(F32)
        local = jnp.clip(target - first, -1.0, float(capacity)).astype(BF16)
        hit = jnp.where(slots == local, jnp.ones_like(slots), jnp.zeros_like(slots))
        return dot(hit, values).astype(BF16)

    def row_copy(kind, offset):
        source, landing = send_rows.at[offset], got_rows.at[offset]
        if kind:
            source, landing = send_half.at[kind - 1, offset], got_half.at[kind - 1, offset]
        return pltpu.make_async_remote_copy(
            src_ref=source,
            dst_ref=landing,
            send_sem=send_sem.at[kind, offset],
            recv_sem=got_sem.at[kind, offset],
            device_id={"grp": other_group(offset)},
            device_id_type=MESH,
        )

    ready = None
    for offset in group_order + [0]:
        send_rows[offset] = place(scaled, offset)
        if ready is None:
            pl.semaphore_wait(barrier, groups + tiles - 2)
        else:
            row_copy(0, ready).start()
        ready = offset
    ready = None
    for offset in group_order + [0]:
        placed = place(misfit, offset)
        send_half[0, offset] = placed[:, :half]
        send_half[1, offset] = placed[:, half:]
        if ready is not None:
            row_copy(1, ready).start()
        ready = offset
    for offset in group_order:
        row_copy(2, offset).start()

    def center(step, _):
        value_load(step).wait()
        part_rows = pl.ds(pl.multiple_of(step * ROW_TILE, ROW_TILE), ROW_TILE)
        now = values_out[part_rows, :].astype(F32)
        anomaly_out[part_rows, :] = (now - jnp.mean(now, axis=1, keepdims=True)).astype(BF16)
        return 0

    for step in range(value_steps):
        value_load(step).start()
    lax.fori_loop(0, value_steps, center, 0)

    gram = (0, gram_part, gram_pieces, gram_mine, gram_whole)
    crosses = [
        (
            1 + side_half,
            cross_part.at[side_half],
            cross_pieces.at[side_half],
            cross_mine.at[side_half],
            cross_whole.at[side_half],
        )
        for side_half in range(2)
    ]

    def rows_of(mine, tile):
        rows = mine.shape[0]
        return pl.ds(pl.multiple_of(tile * rows, rows), rows)

    def piece_copy(one, offset):
        which, part, pieces, mine, _ = one
        return pltpu.make_async_remote_copy(
            src_ref=part.at[rows_of(mine, other_tile(offset))],
            dst_ref=pieces.at[offset],
            send_sem=piece_send.at[which, offset],
            recv_sem=piece_got.at[which, offset],
            device_id={"tile": other_tile(offset)},
            device_id_type=MESH,
        )

    def whole_copy(one, offset, owner):
        which, _, _, mine, whole = one
        return pltpu.make_async_remote_copy(
            src_ref=mine,
            dst_ref=whole.at[rows_of(mine, owner)],
            send_sem=whole_send.at[which, offset],
            recv_sem=whole_got.at[which, offset],
            device_id={"tile": other_tile(offset)},
            device_id_type=MESH,
        )

    def add_up(kind):
        other = send_half.at[kind - 1] if kind else send_rows
        total = dot_rows(send_rows[0], other[0])
        other = got_half.at[kind - 1] if kind else got_rows
        for offset in group_order:
            row_copy(kind, offset).wait_recv()
            total = total + dot_rows(got_rows[offset], other[offset])
        return total

    def send_pieces(one):
        for offset in tile_order:
            piece_copy(one, offset).start()

    def spread(one):
        _, part, pieces, mine, whole = one
        total = part[rows_of(mine, my_tile)]
        for offset in tile_order[::-1]:
            piece_copy(one, offset).wait_recv()
            total = total + pieces[offset]
        mine[...] = total
        whole[rows_of(mine, my_tile)] = total
        for offset in tile_order:
            whole_copy(one, offset, my_tile).start()

    def finish(one):
        for offset in tile_order[::-1]:
            whole_copy(one, offset, other_tile(offset, -1)).wait_recv()

    total = add_up(0)
    gram_part[0:half] = total[:half, :half]
    gram_part[half : 2 * half] = total[:half, half:]
    gram_part[2 * half :] = total[half:, half:]
    send_pieces(gram)
    cross_part[0] = add_up(1)
    send_pieces(crosses[0])
    cross_part[1] = add_up(2)
    send_pieces(crosses[1])
    spread(gram)
    spread(crosses[0])

    spread(crosses[1])
    finish(gram)
    gram_out[:half, :half] = gram_whole[0:half]
    gram_out[:half, half:] = gram_whole[half : 2 * half]
    gram_out[half:, :half] = gram_whole[half : 2 * half].T
    gram_out[half:, half:] = gram_whole[2 * half :]

    identity = (
        lax.broadcasted_iota(jnp.int32, (members, members), 0)
        == lax.broadcasted_iota(jnp.int32, (members, members), 1)
    ).astype(F32)
    matrix = gram_out[...] + identity
    bound = jnp.max(jnp.sum(jnp.abs(matrix), axis=1, keepdims=True), axis=0, keepdims=True)
    bound_out[...] = jnp.broadcast_to(bound, bound_out.shape)

    low_end, high_end = jnp.ones_like(bound), bound
    for step in range(STEPS):
        scale = 2.0 / (low_end + high_end)
        low_end = scale * low_end * (2.0 - scale * low_end)
        high_end = jnp.ones_like(bound)
        if step == 0:
            factor = 2.0 * scale * identity - (scale * scale) * matrix
            pair[:members] = factor
            high, low = split(factor)
            pair[members:] = dot_split(matrix, high, low)
        else:
            factor = 2.0 * scale * identity - (scale * scale) * pair[members:]
            high, low = split(factor)
            if step == STEPS - 1:
                inverse_out[...] = dot_split(pair[:members], high, low)
            else:
                pair[...] = dot_split(pair[...], high, low)

    for side_half, one in enumerate(crosses):
        finish(one)
        cross_out[:, side_half * half : (side_half + 1) * half] = cross_whole[side_half]
    for kind in range(3):
        for offset in group_order:
            row_copy(kind, offset).wait_send()
    for one in [gram] + crosses:
        for offset in tile_order:
            piece_copy(one, offset).wait_send()
            whole_copy(one, offset, my_tile).wait_send()


def sums(groups, tiles, position, bucket, sigma, field, observed, coefficients):
    cells, members = field.shape
    sensors = position.shape[1]
    capacity = sensors // 4
    half = members // 2
    square = jax.ShapeDtypeStruct((members, members), F32)
    ensemble = jax.ShapeDtypeStruct(coefficients.shape, coefficients.dtype)
    inputs = (position, bucket, sigma, field, observed, coefficients)
    return pl.pallas_call(
        functools.partial(exchange, groups, tiles),
        out_shape=[square, square, square, jax.ShapeDtypeStruct((8, 128), F32)]
        + [ensemble] * 2,
        in_specs=[HBM] * 6,
        out_specs=[VMEM] * 6,
        scratch_shapes=[
            pltpu.VMEM((1, sensors), jnp.int32),
            pltpu.VMEM((1, sensors), jnp.int32),
            pltpu.VMEM((1, sensors), F32),
            pltpu.VMEM((sensors, members), BF16),
            pltpu.VMEM((cells, members), BF16),
            pltpu.VMEM((sensors, members), F32),
            pltpu.VMEM((groups, capacity, members), BF16),
            pltpu.VMEM((groups, capacity, members), BF16),
            pltpu.VMEM((2, groups, capacity, half), BF16),
            pltpu.VMEM((2, groups, capacity, half), BF16),
            pltpu.VMEM((3 * half, half), F32),
            pltpu.VMEM((tiles, 3 * half // tiles, half), F32),
            pltpu.VMEM((3 * half // tiles, half), F32),
            pltpu.VMEM((3 * half, half), F32),
            pltpu.VMEM((2, members, half), F32),
            pltpu.VMEM((2, tiles, members // tiles, half), F32),
            pltpu.VMEM((2, members // tiles, half), F32),
            pltpu.VMEM((2, members, half), F32),
            pltpu.VMEM((2 * members, members), F32),
            pltpu.SemaphoreType.DMA((4,)),
            pltpu.SemaphoreType.DMA((cells // BLOCK,)),
            pltpu.SemaphoreType.DMA((coefficients.shape[0] // ROW_TILE,)),
            pltpu.SemaphoreType.DMA((3, groups)),
            pltpu.SemaphoreType.DMA((3, groups)),
            pltpu.SemaphoreType.DMA((3, tiles)),
            pltpu.SemaphoreType.DMA((3, tiles)),
            pltpu.SemaphoreType.DMA((3, tiles)),
            pltpu.SemaphoreType.DMA((3, tiles)),
        ],
        compiler_params=pltpu.CompilerParams(
            collective_id=0, has_side_effects=True, vmem_limit_bytes=16 << 20
        ),
        cost_estimate=pl.CostEstimate(
            flops=4 << 30, bytes_accessed=100 << 20, transcendentals=0
        ),
        name="sums",
    )(*(pltpu.with_memory_space_constraint(x, pltpu.HBM) for x in inputs))


def apply(ready, gram, cross, bound, values, anomaly, out, stored, inverse, transform, store_sem):
    total_rows, members = values.shape
    steps = total_rows // STORE_TILE
    safe = bound[0, 0] <= SAFE_BOUND

    def finish(matrix):
        high, low = split(cross[...])
        weights = dot_split(matrix, high, low)
        transform[...] = (weights / math.sqrt(members - 1)).astype(BF16)

    @pl.when(safe)
    def _():
        finish(ready[...])

    @pl.when(jnp.logical_not(safe))
    def _():
        down = lax.broadcasted_iota(jnp.int32, (members, members), 0)
        along = lax.broadcasted_iota(jnp.int32, (members, members), 1)
        inverse[...] = gram[...] + (down == along).astype(F32)
        line = lax.broadcasted_iota(jnp.int32, (members, 1), 0)
        spot = lax.broadcasted_iota(jnp.int32, (1, members), 1)

        def eliminate(step, _):
            now = inverse[...]
            here, there = (line == step), (spot == step)
            row = jnp.sum(jnp.where(here, now, 0.0), axis=0, keepdims=True)
            column = jnp.sum(jnp.where(there, now, 0.0), axis=1, keepdims=True)
            pivot = jnp.sum(jnp.where(there, row, 0.0), axis=1, keepdims=True)
            row = jnp.where(there, 1.0, row) / pivot
            column = jnp.where(here, 0.0, column)
            base = jnp.where(there, 0.0, now)
            inverse[...] = jnp.where(here, row, base - column * row)
            return 0

        lax.fori_loop(0, members, eliminate, 0)
        finish(inverse[...])

    def store(step):
        rows = pl.ds(step * STORE_TILE, STORE_TILE)
        return pltpu.make_async_copy(stored.at[rows], out.at[rows], store_sem.at[step])

    for step in range(steps):
        rows = pl.ds(step * STORE_TILE, STORE_TILE)
        change = dot(anomaly[rows, :], transform[...])
        stored[rows, :] = (values[rows, :].astype(F32) + change).astype(BF16)
        store(step).start()
    for step in range(steps):
        store(step).wait()


def update(inverse, gram, cross, bound, values, anomaly):
    total_rows, members = values.shape
    return pl.pallas_call(
        apply,
        out_shape=jax.ShapeDtypeStruct(values.shape, values.dtype),
        in_specs=[VMEM] * 6,
        out_specs=HBM,
        scratch_shapes=[
            pltpu.VMEM((total_rows, members), BF16),
            pltpu.VMEM((members, members), F32),
            pltpu.VMEM((members, members), BF16),
            pltpu.SemaphoreType.DMA((total_rows // STORE_TILE,)),
        ],
        compiler_params=pltpu.CompilerParams(vmem_limit_bytes=16 << 20),
        name="update",
    )(inverse, gram, cross, bound, values, anomaly)


def solution(mesh):
    groups, tiles = mesh.shape["grp"], mesh.shape["tile"]

    def shards(coefficients, field, position, bucket, sigma, observed):
        sensors = position.shape[0]
        solved = sums(
            groups,
            tiles,
            position.reshape(1, sensors),
            bucket.reshape(1, sensors),
            sigma.reshape(1, sensors),
            field,
            observed,
            coefficients,
        )
        return update(*solved)

    rows, flat = P(("grp", "tile"), None), P(("grp", "tile"))
    return jax.shard_map(
        shards,
        mesh=mesh,
        in_specs=(rows, rows, flat, rows, flat, rows),
        out_specs=rows,
        check_vma=False,
    )
```

```python
import functools
import math

import jax
import jax.numpy as jnp
from jax import lax
from jax.experimental import pallas as pl
from jax.experimental.pallas import tpu as pltpu
from jax.sharding import PartitionSpec as P

F32, BF16 = jnp.float32, jnp.bfloat16
MESH = pl.DeviceIdType.MESH
VMEM = pl.BlockSpec(memory_space=pltpu.VMEM)
HBM = pl.BlockSpec(memory_space=pltpu.HBM)
BLOCK = 2048
LANES = 128
SAFE_BOUND = 256.0
STEPS = 7
ROW_TILE = 2048
STORE_TILE = 1024


def dot(a, b):
    return lax.dot_general(a, b, (((1,), (0,)), ((), ())), preferred_element_type=F32)


def dot_rows(a, b):
    return lax.dot_general(a, b, (((0,), (0,)), ((), ())), preferred_element_type=F32)


def split(a):
    high = a.astype(BF16)
    return high, (a - high.astype(F32)).astype(BF16)


def dot_split(a, b_high, b_low):
    a_high, a_low = split(a)
    return dot(a_high, b_high) + (dot(a_low, b_high) + dot(a_high, b_low))


def exchange(
    groups,
    tiles,
    position,
    bucket,
    sigma,
    field,
    observed,
    coefficients,
    inverse_out,
    gram_out,
    cross_out,
    bound_out,
    values_out,
    anomaly_out,
    position_vmem,
    bucket_vmem,
    sigma_vmem,
    observed_vmem,
    field_vmem,
    picked,
    send_rows,
    got_rows,
    send_half,
    got_half,
    gram_part,
    gram_pieces,
    gram_mine,
    gram_whole,
    cross_part,
    cross_pieces,
    cross_mine,
    cross_whole,
    pair,
    small_sem,
    field_sem,
    value_sem,
    send_sem,
    got_sem,
    piece_send,
    piece_got,
    whole_send,
    whole_got,
):
    cells, members = field.shape
    sensors = position.shape[1]
    capacity = sensors // 4
    half = members // 2
    root_scale = math.sqrt(members - 1)
    my_group, my_tile = lax.axis_index("grp"), lax.axis_index("tile")
    ys, side = groups // 2, math.isqrt(tiles)

    def other_group(offset):
        far, core = offset // 2, offset % 2
        there = lax.rem(my_group // 2 + far, ys)
        return there * 2 + lax.rem(my_group + core, 2)

    def other_tile(offset, sign=1):
        far, near = offset // side, offset % side
        far, near = (far, near) if sign > 0 else (side - far, side - near)
        z = lax.rem(my_tile // side + far, side)
        return z * side + lax.rem(lax.rem(my_tile, side) + near, side)

    def ring(step, size):
        return min(step, size - step)

    tile_order = sorted(
        range(1, tiles), key=lambda o: -ring(o // side, side) - ring(o % side, side)
    )
    group_order = sorted(range(1, groups), key=lambda o: -ring(o // 2, ys))

    small = [
        pltpu.make_async_copy(source, landing, small_sem.at[number])
        for number, (source, landing) in enumerate(
            (
                (position, position_vmem),
                (bucket, bucket_vmem),
                (sigma, sigma_vmem),
                (observed, observed_vmem),
            )
        )
    ]
    for copy in small[:3]:
        copy.start()
    loads = []
    for block in range(cells // BLOCK):
        part_rows = pl.ds(block * BLOCK, BLOCK)
        loads.append(
            pltpu.make_async_copy(field.at[part_rows], field_vmem.at[part_rows], field_sem.at[block])
        )
        loads[-1].start()
    small[3].start()

    def value_load(step):
        part_rows = pl.ds(pl.multiple_of(step * ROW_TILE, ROW_TILE), ROW_TILE)
        return pltpu.make_async_copy(
            coefficients.at[part_rows], values_out.at[part_rows], value_sem.at[step]
        )

    value_steps = coefficients.shape[0] // ROW_TILE

    barrier = pltpu.get_barrier_semaphore()
    for offset in group_order:
        pl.semaphore_signal(
            barrier, inc=1, device_id={"grp": other_group(offset)}, device_id_type=MESH
        )
    for offset in tile_order:
        pl.semaphore_signal(
            barrier, inc=1, device_id={"tile": other_tile(offset)}, device_id_type=MESH
        )

    lane = lax.broadcasted_iota(jnp.int32, (sensors, sensors), 1)
    row = lax.broadcasted_iota(jnp.int32, (sensors, sensors), 0)
    earlier = (row < lane).astype(F32).astype(BF16)
    for copy in small[:3]:
        copy.wait()
    cell = position_vmem[...].astype(F32)
    block_of = jnp.floor(cell * (1.0 / LANES))
    inverse_sigma = 1.0 / sigma_vmem[...]
    facts = jnp.concatenate(
        [
            block_of,
            cell - block_of * LANES,
            inverse_sigma,
            inverse_sigma * (1.0 / root_scale),
            jnp.zeros((4, sensors), F32),
        ],
        axis=0,
    ).T
    block_column = jnp.broadcast_to(facts[:, 0:1], (sensors, LANES)).astype(BF16)
    spots = lax.broadcasted_iota(jnp.int32, (sensors, LANES), 1).astype(F32)
    spot_hit = (spots == facts[:, 1:2]).astype(F32).astype(BF16)
    none = jnp.zeros_like(spot_hit)

    value = None
    for block in range(cells // BLOCK):
        chosen = jnp.concatenate(
            [
                jnp.where(block_column == float(block * (BLOCK // LANES) + k), spot_hit, none)
                for k in range(BLOCK // LANES)
            ],
            axis=1,
        )
        loads[block].wait()
        more = dot(chosen, field_vmem[pl.ds(block * BLOCK, BLOCK), :])
        value = more if value is None else value + more
    picked[...] = value

    group = bucket_vmem[...]
    member_of = (lax.broadcasted_iota(jnp.int32, (groups, sensors), 0) == group).astype(F32)
    before = dot(member_of.astype(BF16), earlier)
    rank = jnp.sum(before * member_of, axis=0, keepdims=True)
    target = group.astype(F32) * capacity + rank

    kept = picked[...]
    mean = jnp.mean(kept, axis=1, keepdims=True)
    scaled = ((kept - mean) * facts[:, 3:4]).astype(BF16)
    small[3].wait()
    misfit = ((observed_vmem[...].astype(F32) - kept) * facts[:, 2:3]).astype(BF16)

    slots = lax.broadcasted_iota(jnp.int32, (capacity, sensors), 0).astype(F32).astype(BF16)

    def place(values, offset):
        first = (other_group(offset) * capacity).astype(F32)
        local = jnp.clip(target - first, -1.0, float(capacity)).astype(BF16)
        hit = jnp.where(slots == local, jnp.ones_like(slots), jnp.zeros_like(slots))
        return dot(hit, values).astype(BF16)

    def row_copy(kind, offset):
        source, landing = send_rows.at[offset], got_rows.at[offset]
        if kind:
            source, landing = send_half.at[kind - 1, offset], got_half.at[kind - 1, offset]
        return pltpu.make_async_remote_copy(
            src_ref=source,
            dst_ref=landing,
            send_sem=send_sem.at[kind, offset],
            recv_sem=got_sem.at[kind, offset],
            device_id={"grp": other_group(offset)},
            device_id_type=MESH,
        )

    ready = None
    for offset in group_order + [0]:
        send_rows[offset] = place(scaled, offset)
        if ready is None:
            pl.semaphore_wait(barrier, groups + tiles - 2)
        else:
            row_copy(0, ready).start()
        ready = offset
    ready = None
    for offset in group_order + [0]:
        placed = place(misfit, offset)
        send_half[0, offset] = placed[:, :half]
        send_half[1, offset] = placed[:, half:]
        if ready is not None:
            row_copy(1, ready).start()
        ready = offset
    for offset in group_order:
        row_copy(2, offset).start()

    def center(step, _):
        value_load(step).wait()
        part_rows = pl.ds(pl.multiple_of(step * ROW_TILE, ROW_TILE), ROW_TILE)
        now = values_out[part_rows, :].astype(F32)
        anomaly_out[part_rows, :] = (now - jnp.mean(now, axis=1, keepdims=True)).astype(BF16)
        return 0

    for step in range(value_steps):
        value_load(step).start()
    lax.fori_loop(0, value_steps, center, 0)

    gram = (0, gram_part, gram_pieces, gram_mine, gram_whole)
    crosses = [
        (
            1 + side_half,
            cross_part.at[side_half],
            cross_pieces.at[side_half],
            cross_mine.at[side_half],
            cross_whole.at[side_half],
        )
        for side_half in range(2)
    ]

    def rows_of(mine, tile):
        rows = mine.shape[0]
        return pl.ds(pl.multiple_of(tile * rows, rows), rows)

    def piece_copy(one, offset):
        which, part, pieces, mine, _ = one
        return pltpu.make_async_remote_copy(
            src_ref=part.at[rows_of(mine, other_tile(offset))],
            dst_ref=pieces.at[offset],
            send_sem=piece_send.at[which, offset],
            recv_sem=piece_got.at[which, offset],
            device_id={"tile": other_tile(offset)},
            device_id_type=MESH,
        )

    def whole_copy(one, offset, owner):
        which, _, _, mine, whole = one
        return pltpu.make_async_remote_copy(
            src_ref=mine,
            dst_ref=whole.at[rows_of(mine, owner)],
            send_sem=whole_send.at[which, offset],
            recv_sem=whole_got.at[which, offset],
            device_id={"tile": other_tile(offset)},
            device_id_type=MESH,
        )

    def add_up(kind):
        other = send_half.at[kind - 1] if kind else send_rows
        total = dot_rows(send_rows[0], other[0])
        other = got_half.at[kind - 1] if kind else got_rows
        for offset in group_order:
            row_copy(kind, offset).wait_recv()
            total = total + dot_rows(got_rows[offset], other[offset])
        return total

    def send_pieces(one):
        for offset in tile_order:
            piece_copy(one, offset).start()

    def spread(one):
        _, part, pieces, mine, whole = one
        total = part[rows_of(mine, my_tile)]
        for offset in tile_order[::-1]:
            piece_copy(one, offset).wait_recv()
            total = total + pieces[offset]
        mine[...] = total
        whole[rows_of(mine, my_tile)] = total
        for offset in tile_order:
            whole_copy(one, offset, my_tile).start()

    def finish(one):
        for offset in tile_order[::-1]:
            whole_copy(one, offset, other_tile(offset, -1)).wait_recv()

    total = add_up(0)
    gram_part[0:half] = total[:half, :half]
    gram_part[half : 2 * half] = total[:half, half:]
    gram_part[2 * half :] = total[half:, half:]
    send_pieces(gram)
    cross_part[0] = add_up(1)
    send_pieces(crosses[0])
    cross_part[1] = add_up(2)
    send_pieces(crosses[1])
    spread(gram)
    spread(crosses[0])

    spread(crosses[1])
    finish(gram)
    gram_out[:half, :half] = gram_whole[0:half]
    gram_out[:half, half:] = gram_whole[half : 2 * half]
    gram_out[half:, :half] = gram_whole[half : 2 * half].T
    gram_out[half:, half:] = gram_whole[2 * half :]

    identity = (
        lax.broadcasted_iota(jnp.int32, (members, members), 0)
        == lax.broadcasted_iota(jnp.int32, (members, members), 1)
    ).astype(F32)
    matrix = gram_out[...] + identity
    bound = jnp.max(jnp.sum(jnp.abs(matrix), axis=1, keepdims=True), axis=0, keepdims=True)
    bound_out[...] = jnp.broadcast_to(bound, bound_out.shape)

    low_end, high_end = jnp.ones_like(bound), bound
    for step in range(STEPS):
        scale = 2.0 / (low_end + high_end)
        low_end = scale * low_end * (2.0 - scale * low_end)
        high_end = jnp.ones_like(bound)
        if step == 0:
            factor = 2.0 * scale * identity - (scale * scale) * matrix
            pair[:members] = factor
            high, low = split(factor)
            pair[members:] = dot_split(matrix, high, low)
        else:
            factor = 2.0 * scale * identity - (scale * scale) * pair[members:]
            high, low = split(factor)
            if step == STEPS - 1:
                inverse_out[...] = dot_split(pair[:members], high, low)
            else:
                pair[...] = dot_split(pair[...], high, low)

    for side_half, one in enumerate(crosses):
        finish(one)
        cross_out[:, side_half * half : (side_half + 1) * half] = cross_whole[side_half]
    for kind in range(3):
        for offset in group_order:
            row_copy(kind, offset).wait_send()
    for one in [gram] + crosses:
        for offset in tile_order:
            piece_copy(one, offset).wait_send()
            whole_copy(one, offset, my_tile).wait_send()


def sums(groups, tiles, position, bucket, sigma, field, observed, coefficients):
    cells, members = field.shape
    sensors = position.shape[1]
    capacity = sensors // 4
    half = members // 2
    square = jax.ShapeDtypeStruct((members, members), F32)
    ensemble = jax.ShapeDtypeStruct(coefficients.shape, coefficients.dtype)
    inputs = (position, bucket, sigma, field, observed, coefficients)
    return pl.pallas_call(
        functools.partial(exchange, groups, tiles),
        out_shape=[square, square, square, jax.ShapeDtypeStruct((8, 128), F32)]
        + [ensemble] * 2,
        in_specs=[HBM] * 6,
        out_specs=[VMEM] * 6,
        scratch_shapes=[
            pltpu.VMEM((1, sensors), jnp.int32),
            pltpu.VMEM((1, sensors), jnp.int32),
            pltpu.VMEM((1, sensors), F32),
            pltpu.VMEM((sensors, members), BF16),
            pltpu.VMEM((cells, members), BF16),
            pltpu.VMEM((sensors, members), F32),
            pltpu.VMEM((groups, capacity, members), BF16),
            pltpu.VMEM((groups, capacity, members), BF16),
            pltpu.VMEM((2, groups, capacity, half), BF16),
            pltpu.VMEM((2, groups, capacity, half), BF16),
            pltpu.VMEM((3 * half, half), F32),
            pltpu.VMEM((tiles, 3 * half // tiles, half), F32),
            pltpu.VMEM((3 * half // tiles, half), F32),
            pltpu.VMEM((3 * half, half), F32),
            pltpu.VMEM((2, members, half), F32),
            pltpu.VMEM((2, tiles, members // tiles, half), F32),
            pltpu.VMEM((2, members // tiles, half), F32),
            pltpu.VMEM((2, members, half), F32),
            pltpu.VMEM((2 * members, members), F32),
            pltpu.SemaphoreType.DMA((4,)),
            pltpu.SemaphoreType.DMA((cells // BLOCK,)),
            pltpu.SemaphoreType.DMA((coefficients.shape[0] // ROW_TILE,)),
            pltpu.SemaphoreType.DMA((3, groups)),
            pltpu.SemaphoreType.DMA((3, groups)),
            pltpu.SemaphoreType.DMA((3, tiles)),
            pltpu.SemaphoreType.DMA((3, tiles)),
            pltpu.SemaphoreType.DMA((3, tiles)),
            pltpu.SemaphoreType.DMA((3, tiles)),
        ],
        compiler_params=pltpu.CompilerParams(
            collective_id=0, has_side_effects=True, vmem_limit_bytes=16 << 20
        ),
        cost_estimate=pl.CostEstimate(
            flops=4 << 30, bytes_accessed=100 << 20, transcendentals=0
        ),
        name="sums",
    )(*(pltpu.with_memory_space_constraint(x, pltpu.HBM) for x in inputs))


def apply(ready, gram, cross, bound, values, anomaly, out, stored, inverse, transform, store_sem):
    total_rows, members = values.shape
    steps = total_rows // STORE_TILE
    safe = bound[0, 0] <= SAFE_BOUND

    def finish(weights):
        transform[...] = (weights / math.sqrt(members - 1)).astype(BF16)

    @pl.when(safe)
    def _():
        high, low = split(cross[...])
        finish(dot_split(ready[...], high, low))

    @pl.when(jnp.logical_not(safe))
    def _():
        down = lax.broadcasted_iota(jnp.int32, (members, members), 0)
        along = lax.broadcasted_iota(jnp.int32, (members, members), 1)
        inverse[...] = gram[...] + (down == along).astype(F32)
        line = lax.broadcasted_iota(jnp.int32, (members, 1), 0)
        spot = lax.broadcasted_iota(jnp.int32, (1, members), 1)

        def eliminate(step, _):
            now = inverse[...]
            here, there = (line == step), (spot == step)
            row = jnp.sum(jnp.where(here, now, 0.0), axis=0, keepdims=True)
            column = jnp.sum(jnp.where(there, now, 0.0), axis=1, keepdims=True)
            pivot = jnp.sum(jnp.where(there, row, 0.0), axis=1, keepdims=True)
            row = jnp.where(there, 1.0, row) / pivot
            column = jnp.where(here, 0.0, column)
            base = jnp.where(there, 0.0, now)
            inverse[...] = jnp.where(here, row, base - column * row)
            return 0

        lax.fori_loop(0, members, eliminate, 0)
        finish(
            jnp.dot(
                inverse[...],
                cross[...],
                precision=lax.Precision.HIGHEST,
                preferred_element_type=F32,
            )
        )

    def store(step):
        rows = pl.ds(step * STORE_TILE, STORE_TILE)
        return pltpu.make_async_copy(stored.at[rows], out.at[rows], store_sem.at[step])

    for step in range(steps):
        rows = pl.ds(step * STORE_TILE, STORE_TILE)
        change = dot(anomaly[rows, :], transform[...])
        stored[rows, :] = (values[rows, :].astype(F32) + change).astype(BF16)
        store(step).start()
    for step in range(steps):
        store(step).wait()


def update(inverse, gram, cross, bound, values, anomaly):
    total_rows, members = values.shape
    return pl.pallas_call(
        apply,
        out_shape=jax.ShapeDtypeStruct(values.shape, values.dtype),
        in_specs=[VMEM] * 6,
        out_specs=HBM,
        scratch_shapes=[
            pltpu.VMEM((total_rows, members), BF16),
            pltpu.VMEM((members, members), F32),
            pltpu.VMEM((members, members), BF16),
            pltpu.SemaphoreType.DMA((total_rows // STORE_TILE,)),
        ],
        compiler_params=pltpu.CompilerParams(vmem_limit_bytes=16 << 20),
        name="update",
    )(inverse, gram, cross, bound, values, anomaly)


def solution(mesh):
    groups, tiles = mesh.shape["grp"], mesh.shape["tile"]

    def shards(coefficients, field, position, bucket, sigma, observed):
        sensors = position.shape[0]
        solved = sums(
            groups,
            tiles,
            position.reshape(1, sensors),
            bucket.reshape(1, sensors),
            sigma.reshape(1, sensors),
            field,
            observed,
            coefficients,
        )
        return update(*solved)

    rows, flat = P(("grp", "tile"), None), P(("grp", "tile"))
    return jax.shard_map(
        shards,
        mesh=mesh,
        in_specs=(rows, rows, flat, rows, flat, rows),
        out_specs=rows,
        check_vma=False,
    )
```
